128 devices in a mesh: dev: 16 (over y, x_hi, core), ta: 8 (over x_lo, z).
Axes of the slice: x: 4 (x_hi: 2, x_lo: 2; x = x_hi * 2 + x_lo), y: 4, z: 4, core: 2. Of those that a mesh axis runs over, the one named last changes fastest.
Arguments:
- tokens: bfloat16 [8, 32, 144, 384], P('ta', 'dev'), may hold values from -36 to 36
- out_grad: bfloat16 [8, 32, 144, 384], P('ta', 'dev'), may hold values from -6 to 6
- first_gain: float32 [384], replicated, may hold values from 0.25 to 1.75
- depth_qkv: bfloat16 [384, 1152], replicated, may hold values from -0.3125 to 0.3125
- depth_out: bfloat16 [384, 384], replicated, may hold values from -0.3125 to 0.3125
- time_qkv: bfloat16 [384, 1152], replicated, may hold values from -0.3125 to 0.3125
- time_out: bfloat16 [384, 384], replicated, may hold values from -0.3125 to 0.3125
- second_gain: float32 [384], replicated, may hold values from 0.25 to 1.75
- up_weight: bfloat16 [384, 1536], replicated, may hold values from -0.3125 to 0.3125
- spatial_kernel: float32 [3, 3, 3, 1536], replicated, may hold values from -1.25 to 1.25
- down_weight: bfloat16 [1536, 384], replicated, may hold values from -0.15625 to 0.15625
- depth_scale: float32 [6], replicated, may hold values from 2 to 10
- time_scale: float32 [6], replicated, may hold values from 2 to 10
Outputs:
- block_out: bfloat16 [8, 32, 144, 384], P('ta', 'dev')
- input_grad: bfloat16 [8, 32, 144, 384], P('ta', 'dev')
- depth_qkv_grad: float32 [384, 1152], replicated
- depth_out_grad: float32 [384, 384], replicated
- time_qkv_grad: float32 [384, 1152], replicated
- time_out_grad: float32 [384, 384], replicated
- up_grad: float32 [384, 1536], replicated
- kernel_grad: float32 [3, 3, 3, 1536], replicated
- down_grad: float32 [1536, 384], replicated
- first_gain_grad: float32 [384], replicated
- second_gain_grad: float32 [384], replicated
- depth_scale_grad: float32 [6], replicated
- time_scale_grad: float32 [6], replicated
The draws below stay inside these ranges and needn't reach their ends.
All inputs are finite; a program needn't handle non-finite values.
Results may differ from the reference program's by a relative error of at most 0.015.
Values may be sent and summed in bfloat16 or wider, within the bound.
No kernel may reach another device: no remote copies, remote signals or barrier semaphores. Data moves between devices by JAX's collectives and lax.ppermute only.
A program may use at most 128 MiB of HBM per device.

```python
import math
import jax
import jax.numpy as jnp
from jax import lax

C = 384
NH = 6
HID = 1536
PH = 6
PW = 24
CELLS = 144
DEPTH = 32
FRAMES = 8


def draw_tokens(key, part):
    key_base, key_rows, key_cols = jax.random.split(key, 3)
    shape = (FRAMES, DEPTH, PH * PW, C)
    row_scale = jnp.exp(jax.random.uniform(key_rows, (FRAMES, DEPTH, PH * PW, 1), jnp.float32, math.log(0.3), math.log(3.0)))
    col_scale = jnp.exp(jax.random.uniform(key_cols, (C,), jnp.float32, math.log(0.3), math.log(3.0)))
    base = jax.random.normal(key_base, shape, jnp.float32)
    base = jnp.clip(base, -4.0, 4.0)
    return (base * row_scale * col_scale).astype(jnp.bfloat16)


def steps_of(own_key, dims, pieces, least, largest):
    def one(dim, blocks):
        steps = jax.random.uniform(jax.random.fold_in(jax.random.fold_in(own_key, 6), dim), (blocks,), jnp.float32, least / len(pieces), largest / len(pieces))
        return jnp.repeat(jnp.exp(steps), dims[dim] // blocks).reshape((-1,) + (1,) * (len(dims) - dim - 1))

    loudness = one(*pieces[0])
    for cut in pieces[1:]:
        loudness = loudness * one(*cut)
    return loudness


def scatter_about(stream_key, shape, scale, limit, pieces=(), kind=jnp.bfloat16):
    array = jax.random.normal(stream_key, shape, jnp.float32) * scale
    if len(pieces) > 0:
        array = steps_of(stream_key, shape, pieces, -0.22, 0.18) * array
    return jnp.clip(array, min=-limit, max=limit).astype(kind)


def setup_inputs(seed: int = 0) -> dict:
    key_list = jax.random.split(jax.random.key(seed), 14)
    return {
        "tokens": draw_tokens(jax.random.fold_in(key_list[13], 71), 0),
        "out_grad": scatter_about(key_list[1], (FRAMES, DEPTH, CELLS, C), 1.0, 6.0, ((0, 8), (1, 16))),
        "first_gain": jnp.clip(1.0 + 0.15 * jax.random.normal(key_list[2], (C,), jnp.float32), 0.25, 1.75),
        "depth_qkv": scatter_about(key_list[3], (C, 3 * C), C ** -0.5, 0.3125),
        "depth_out": scatter_about(key_list[4], (C, C), C ** -0.5, 0.3125),
        "time_qkv": scatter_about(key_list[5], (C, 3 * C), C ** -0.5, 0.3125),
        "time_out": scatter_about(key_list[6], (C, C), C ** -0.5, 0.3125),
        "second_gain": jnp.clip(1.0 + 0.15 * jax.random.normal(key_list[7], (C,), jnp.float32), 0.25, 1.75),
        "up_weight": scatter_about(key_list[8], (C, HID), C ** -0.5, 0.3125),
        "spatial_kernel": scatter_about(key_list[9], (3, 3, 3, HID), 27 ** -0.5, 1.25, (), jnp.float32),
        "down_weight": scatter_about(key_list[10], (HID, C), HID ** -0.5, 0.15625),
        "depth_scale": jnp.clip(jnp.exp(jax.random.uniform(key_list[11], (NH,), jnp.float32, math.log(2.0), math.log(10.0))), 2.0, 10.0),
        "time_scale": jnp.clip(jnp.exp(jax.random.uniform(key_list[12], (NH,), jnp.float32, math.log(2.0), math.log(10.0))), 2.0, 10.0),
    }


def rounded(values):
    return lax.optimization_barrier(values.astype(jnp.bfloat16))

def normalize(values, gain):
    centered = values - lax.optimization_barrier(jnp.mean(values, axis=-1, keepdims=True))
    spread = lax.optimization_barrier(jnp.mean(centered * centered, axis=-1, keepdims=True))
    return centered * lax.rsqrt(spread + 1e-05) * gain

def project(left, weight):
    return jnp.dot(left, weight, preferred_element_type=jnp.float32)

def back_project(grads, weight):
    return lax.dot_general(grads, weight, (((grads.ndim - 1,), (1,)), ((), ())), preferred_element_type=jnp.float32)

def weight_grad(left, grads):
    lead = tuple(range(left.ndim - 1))
    return lax.dot_general(left, grads, ((lead, lead), ((), ())), preferred_element_type=jnp.float32)

def attend(fields, scale):
    width = fields.shape[-1] // 3
    heads = scale.shape[0]
    split_shape = fields.shape[:-1] + (heads, width // heads)
    query = fields[..., :width].reshape(split_shape)
    keyed = fields[..., width:2 * width].reshape(split_shape)
    valued = fields[..., 2 * width:].reshape(split_shape)
    query = query * lax.rsqrt(lax.optimization_barrier(jnp.sum(query * query, axis=-1, keepdims=True)) + 1e-06)
    keyed = keyed * lax.rsqrt(lax.optimization_barrier(jnp.sum(keyed * keyed, axis=-1, keepdims=True)) + 1e-06)
    scores = jnp.einsum('plbhd,pmbhd->pbhlm', query, keyed, precision=lax.Precision.HIGHEST)
    scores = scores * scale[:, None, None]
    weights = jnp.exp(scores)
    weights = weights / lax.optimization_barrier(jnp.sum(weights, axis=-1, keepdims=True))
    mixed = jnp.einsum('pbhlm,pmbhd->plbhd', weights, valued, precision=lax.Precision.HIGHEST)
    return mixed.reshape(fields.shape[:-1] + (width,))

def activate(values):
    return 0.5 * values * (1.0 + jnp.tanh(0.7978845608 * (values + 0.044715 * values * values * values)))

def filter_forward(padded, kernel):
    depth = padded.shape[1] - 2
    rows = padded.shape[2] - 2
    cols = padded.shape[3] - 2
    total = jnp.zeros((padded.shape[0], depth, rows, cols, padded.shape[4]), jnp.float32)
    for depth_off in range(3):
        for row_off in range(3):
            for col_off in range(3):
                window = padded[:, depth_off:depth_off + depth, row_off:row_off + rows, col_off:col_off + cols]
                total = total + kernel[depth_off, row_off, col_off] * window.astype(jnp.float32)
    return total

def filter_backward(grad_pad, kernel):
    depth = grad_pad.shape[1] - 2
    rows = grad_pad.shape[2] - 2
    cols = grad_pad.shape[3] - 2
    total = jnp.zeros((grad_pad.shape[0], depth, rows, cols, grad_pad.shape[4]), jnp.float32)
    for depth_off in range(3):
        for row_off in range(3):
            for col_off in range(3):
                window = grad_pad[:, 2 - depth_off:2 - depth_off + depth, 2 - row_off:2 - row_off + rows, 2 - col_off:2 - col_off + cols]
                total = total + kernel[depth_off, row_off, col_off] * window.astype(jnp.float32)
    return total

def kernel_terms(padded, grads):
    depth = grads.shape[1]
    rows = grads.shape[2]
    cols = grads.shape[3]
    grads_wide = grads.astype(jnp.float32)
    terms = []
    for depth_off in range(3):
        for row_off in range(3):
            for col_off in range(3):
                window = padded[:, depth_off:depth_off + depth, row_off:row_off + rows, col_off:col_off + cols]
                terms.append(lax.optimization_barrier(jnp.sum(window.astype(jnp.float32) * grads_wide, axis=(0, 1, 2, 3))))
    return jnp.stack(terms).reshape(3, 3, 3, grads.shape[4])

def feed_forward(middle, out_grad, second_gain, up_weight, spatial_kernel, down_weight):
    frames, depth, cells, width = middle.shape
    middle_wide = middle.astype(jnp.float32)
    norm_second = rounded(normalize(middle_wide, second_gain))
    hidden = rounded(project(norm_second, up_weight))
    shaped = hidden.reshape(frames, depth, PH, PW, -1)
    padded = jnp.pad(shaped, ((0, 0), (1, 1), (1, 1), (1, 1), (0, 0)))
    filtered = filter_forward(padded, spatial_kernel)
    activated, act_back = jax.vjp(activate, filtered)
    active = rounded(activated).reshape(frames, depth, cells, -1)
    block_out = rounded(middle_wide + project(active, down_weight))
    down_grad = weight_grad(active, out_grad)
    active_grad = back_project(out_grad, down_weight)
    filtered_grad = rounded(act_back(active_grad.reshape(filtered.shape))[0])
    grad_pad = jnp.pad(filtered_grad, ((0, 0), (1, 1), (1, 1), (1, 1), (0, 0)))
    hidden_grad = rounded(filter_backward(grad_pad, spatial_kernel)).reshape(frames, depth, cells, -1)
    kernel_grad = kernel_terms(padded, filtered_grad)
    up_grad = weight_grad(norm_second, hidden_grad)
    second_back = back_project(hidden_grad, up_weight)
    norm_out, norm_back = jax.vjp(normalize, middle_wide, second_gain)
    middle_part, second_gain_grad = norm_back(second_back)
    middle_grad = out_grad.astype(jnp.float32) + middle_part
    return (block_out, middle_grad, up_grad, kernel_grad, down_grad, second_gain_grad)

def reference(tokens, out_grad, first_gain, depth_qkv, depth_out, time_qkv, time_out, second_gain, up_weight, spatial_kernel, down_weight, depth_scale, time_scale):
    frames, depth, cells, width = tokens.shape
    base = tokens.astype(jnp.float32)
    norm_first = rounded(normalize(base, first_gain))
    depth_fields = rounded(project(norm_first, depth_qkv))
    depth_wide, depth_back = jax.vjp(attend, depth_fields.astype(jnp.float32), depth_scale)
    depth_mixed = rounded(depth_wide)
    time_fields = rounded(project(norm_first, time_qkv)).reshape(1, frames, depth * cells, 3 * width)
    time_wide, time_back = jax.vjp(attend, time_fields.astype(jnp.float32), time_scale)
    time_mixed = rounded(time_wide).reshape(frames, depth, cells, width)
    depth_branch = rounded(project(depth_mixed, depth_out))
    time_branch = rounded(project(time_mixed, time_out))
    middle = rounded(base + depth_branch.astype(jnp.float32) + time_branch.astype(jnp.float32))

    def one_frame(pair):
        results = feed_forward(pair[0][None], pair[1][None], second_gain, up_weight, spatial_kernel, down_weight)
        return (results[0][0], results[1][0], results[2], results[3], results[4], results[5])
    stacked = lax.map(one_frame, (middle, out_grad))
    block_out = stacked[0]
    middle_grad = stacked[1]
    up_grad = lax.optimization_barrier(jnp.sum(stacked[2], axis=0))
    kernel_grad = lax.optimization_barrier(jnp.sum(stacked[3], axis=0))
    down_grad = lax.optimization_barrier(jnp.sum(stacked[4], axis=0))
    second_gain_grad = lax.optimization_barrier(jnp.sum(stacked[5], axis=0))
    branch_grad = rounded(middle_grad)
    depth_out_grad = weight_grad(depth_mixed, branch_grad)
    time_out_grad = weight_grad(time_mixed, branch_grad)
    depth_mixed_grad = rounded(back_project(branch_grad, depth_out))
    time_mixed_grad = rounded(back_project(branch_grad, time_out)).reshape(1, frames, depth * cells, width)
    depth_fields_wide, depth_scale_grad = depth_back(depth_mixed_grad.astype(jnp.float32))
    depth_fields_grad = rounded(depth_fields_wide)
    time_fields_wide, time_scale_grad = time_back(time_mixed_grad.astype(jnp.float32))
    time_fields_grad = rounded(time_fields_wide).reshape(frames, depth, cells, 3 * width)
    depth_qkv_grad = weight_grad(norm_first, depth_fields_grad)
    time_qkv_grad = weight_grad(norm_first, time_fields_grad)
    first_back = rounded(back_project(depth_fields_grad, depth_qkv)).astype(jnp.float32) + rounded(back_project(time_fields_grad, time_qkv)).astype(jnp.float32)
    norm_out, first_norm_back = jax.vjp(normalize, base, first_gain)
    base_grad, first_gain_grad = first_norm_back(first_back)
    input_grad = (middle_grad + base_grad).astype(jnp.bfloat16)
    factor = 1.0 / math.sqrt(frames * depth * cells)
    return (block_out, input_grad, depth_qkv_grad * factor, depth_out_grad * factor, time_qkv_grad * factor, time_out_grad * factor, up_grad * factor, kernel_grad * factor, down_grad * factor, first_gain_grad * factor, second_gain_grad * factor, depth_scale_grad * factor, time_scale_grad * factor)
```

```python
import functools
import math

import jax
import jax.numpy as jnp
import numpy as np
from jax import lax
from jax.experimental import pallas as pl
from jax.experimental.pallas import tpu as pltpu
from jax.sharding import Mesh
from jax.sharding import PartitionSpec as P

C = 384
HID = 1536
PW = 24
CELLS = 144
ROWS = 288
BLOCK = 256
STEPS = HID // BLOCK
PAD = 192
DEV = ("y", "xh", "core")
TA = ("xl", "z")
CHIPS = ("y", "xh", "xl", "z")
COPIES = 64
CHUNK = 152
F32 = jnp.float32
BF16 = jnp.bfloat16
EPS = 1e-5


def spread_depth():
    table = np.zeros((16, 24, ROWS), np.float32)
    for owner in range(16):
        for k in range(18):
            table[owner, k, (k // 9) * CELLS + 9 * owner + k % 9] = 1
    return table.reshape(384, ROWS)


def spread_time():
    table = np.zeros((8, 40, ROWS), np.float32)
    for owner in range(8):
        for k in range(36):
            table[owner, k, (k // 18) * CELLS + 18 * owner + k % 18] = 1
    return table.reshape(320, ROWS)


def groups_depth():
    k = np.arange(384) % 24
    return np.where(k < 18, k % 9, k - 9).astype(np.int32)


def groups_time():
    return (np.arange(320) % 40).astype(np.int32)


def dot(left, right, dims=((1,), (0,)), precision=None):
    return lax.dot_general(
        left, right, (dims, ((), ())), preferred_element_type=F32, precision=precision
    )


def norm_parts(values):
    centered = values - jnp.mean(values, axis=-1, keepdims=True)
    inverse = lax.rsqrt(jnp.mean(centered * centered, axis=-1, keepdims=True) + EPS)
    return centered * inverse, inverse


def norm_back(scaled, inverse, grads):
    mean = jnp.mean(grads, axis=-1, keepdims=True)
    along = jnp.mean(grads * scaled, axis=-1, keepdims=True)
    return (grads - mean - scaled * along) * inverse


def vmem(count):
    return [pl.BlockSpec(memory_space=pltpu.VMEM)] * count


def shape(dims, kind=BF16):
    return jax.ShapeDtypeStruct(dims, kind)


def first_kernel(tok_ref, gain_ref, pd_ref, pt_ref, dep_ref, tim_ref):
    scaled, _ = norm_parts(tok_ref[...].astype(F32))
    normed = (scaled * gain_ref[...]).astype(BF16)
    dep_ref[...] = dot(pd_ref[...], normed).reshape(16, 24, C).astype(BF16)
    tim_ref[...] = dot(pt_ref[...], normed).reshape(8, 40, C).astype(BF16)


def first_norm(tokens, gain, pd, pt):
    return pl.pallas_call(
        first_kernel,
        out_shape=(shape((16, 24, C)), shape((8, 40, C))),
        in_specs=vmem(4),
        out_specs=tuple(vmem(2)),
        name="first_norm",
    )(tokens, gain, pd, pt)


def lane_is_low():
    return lax.broadcasted_iota(jnp.int32, (1, 128), 1) < 64


def head_ones():
    row = lax.broadcasted_iota(jnp.int32, (128, 128), 0) < 64
    col = lax.broadcasted_iota(jnp.int32, (128, 128), 1) < 64
    return jnp.where(row == col, 1.0, 0.0).astype(BF16)


def head_sum(values, ones):
    high = values.astype(BF16)
    low = (values - high.astype(F32)).astype(BF16)
    return dot(high, ones) + dot(low, ones)


def attend_kernel(in_ref, w_ref, wo_ref, scale_ref, gr_ref, gc_ref, out_ref, fields_ref, mixed_ref, same_ref):
    count, part, _ = in_ref.shape
    rows = count * part
    rowed = in_ref[...].astype(F32).reshape(rows, C).astype(BF16)
    fields_ref[...] = dot(rowed, w_ref[...]).astype(BF16)
    same_ref[...] = jnp.where(gr_ref[...] == gc_ref[...], 1.0, 0.0)
    ones = head_ones()
    low = lane_is_low()
    side = jnp.ones((rows, 128), BF16)
    for pair in range(3):
        at = 128 * pair
        query = fields_ref[:, at : at + 128].astype(F32)
        keyed = fields_ref[:, C + at : C + at + 128].astype(F32)
        valued = fields_ref[:, 2 * C + at : 2 * C + at + 128]
        query = query * lax.rsqrt(head_sum(query * query, ones) + 1e-6)
        keyed = (keyed * lax.rsqrt(head_sum(keyed * keyed, ones) + 1e-6)).astype(BF16)
        query = query * jnp.where(low, scale_ref[2 * pair], scale_ref[2 * pair + 1])
        both = jnp.concatenate([valued, side], axis=1)
        results = []
        for half in range(2):
            mine = low if half == 0 else jnp.logical_not(low)
            scores = dot(jnp.where(mine, query, 0.0).astype(BF16), keyed, ((1,), (1,)))
            weights = (jnp.exp(scores) * same_ref[...]).astype(BF16)
            sums = dot(weights, both)
            results.append(sums[:, :128] / sums[:, 128:])
        mixed_ref[:, at : at + 128] = jnp.where(low, results[0], results[1]).astype(BF16)
    out_ref[...] = dot(mixed_ref[...], wo_ref[...]).reshape(count, part, C).astype(BF16)


def attend(inputs, weight, out_weight, scale, groups, name):
    count, part, _ = inputs.shape
    rows = count * part
    return pl.pallas_call(
        attend_kernel,
        out_shape=(shape((count, part, C)), shape((rows, 3 * C)), shape((rows, C))),
        in_specs=vmem(3) + [pl.BlockSpec(memory_space=pltpu.SMEM)] + vmem(2),
        out_specs=tuple(vmem(3)),
        scratch_shapes=[pltpu.VMEM((rows, rows), F32)],
        name=name,
    )(inputs, weight, out_weight, scale, groups[:, None], groups[None, :])


def attend_back_kernel(
    grad_ref, in_ref, fields_ref, mixed_ref, w_ref, wo_ref, scale_ref, gr_ref, gc_ref, gain_ref,
    out_ref, weights_ref, small_ref, same_ref, fg_ref,
):
    count, part, _ = in_ref.shape
    rows = count * part
    grads = grad_ref[...].astype(F32).reshape(rows, C).astype(BF16)
    same_ref[...] = jnp.where(gr_ref[...] == gc_ref[...], 1.0, 0.0)
    out_grad = dot(mixed_ref[...], grads, ((0,), (0,)))
    for tile in range(3):
        weights_ref[9 + tile] = out_grad[:, 128 * tile : 128 * tile + 128].astype(BF16)
    mixed_grad = dot(grads, wo_ref[...], ((1,), (1,))).astype(BF16)
    ones = head_ones()
    low = lane_is_low()
    side = jnp.ones((rows, 128), BF16)
    small_ref[24:32, :] = jnp.zeros((8, 128), F32)
    for pair in range(3):
        at = 128 * pair
        query = fields_ref[:, at : at + 128].astype(F32)
        keyed = fields_ref[:, C + at : C + at + 128].astype(F32)
        valued = fields_ref[:, 2 * C + at : 2 * C + at + 128]
        query_inv = lax.rsqrt(head_sum(query * query, ones) + 1e-6)
        keyed_inv = lax.rsqrt(head_sum(keyed * keyed, ones) + 1e-6)
        query = query * query_inv
        keyed = keyed * keyed_inv
        scale = jnp.where(low, scale_ref[2 * pair], scale_ref[2 * pair + 1])
        scaled = query * scale
        keyed_short = keyed.astype(BF16)
        cot = mixed_grad[:, at : at + 128]
        delta = head_sum(cot.astype(F32) * mixed_ref[:, at : at + 128].astype(F32), ones)
        query_grad = jnp.zeros((rows, 128), F32)
        keyed_grad = jnp.zeros((rows, 128), F32)
        value_grad = jnp.zeros((rows, 128), F32)
        for half in range(2):
            mine = low if half == 0 else jnp.logical_not(low)
            lane = 64 * half
            mine_query = jnp.where(mine, scaled, 0.0).astype(BF16)
            mine_cot = jnp.where(mine, cot.astype(F32), 0.0).astype(BF16)
            mine_keyed = jnp.where(mine, keyed, 0.0).astype(BF16)
            scores = dot(mine_query, keyed_short, ((1,), (1,)))
            weights = jnp.exp(scores) * same_ref[...]
            total = dot(weights.astype(BF16), side)
            weights = weights * (1.0 / total)[:, :1]
            weights_grad = dot(mine_cot, valued, ((1,), (1,)))
            scores_grad = (weights * (weights_grad - delta[:, lane : lane + 1])).astype(BF16)
            value_grad = value_grad + dot(weights.astype(BF16), mine_cot, ((0,), (0,)))
            query_grad = query_grad + dot(scores_grad, mine_keyed)
            keyed_grad = keyed_grad + dot(scores_grad, mine_query, ((0,), (0,)))
        along = jnp.sum(query_grad * query, axis=0, keepdims=True)
        small_ref[24 + pair : 25 + pair, :] = head_sum(jnp.broadcast_to(along, (8, 128)), ones)[:1]
        query_grad = query_grad * scale
        query_grad = (query_grad - query * head_sum(query * query_grad, ones)) * query_inv
        keyed_grad = (keyed_grad - keyed * head_sum(keyed * keyed_grad, ones)) * keyed_inv
        fg_ref[:, at : at + 128] = query_grad.astype(BF16)
        fg_ref[:, C + at : C + at + 128] = keyed_grad.astype(BF16)
        fg_ref[:, 2 * C + at : 2 * C + at + 128] = value_grad.astype(BF16)
    out_ref[...] = dot(fg_ref[...], w_ref[...], ((1,), (1,))).reshape(count, part, C).astype(BF16)
    rowed = in_ref[...].astype(F32).reshape(rows, C).astype(BF16)
    grad = dot(rowed, fg_ref[...], ((0,), (0,)))
    product = jnp.zeros((C, 128), F32)
    for tile in range(9):
        at = 128 * tile
        weights_ref[tile] = grad[:, at : at + 128].astype(BF16)
        product = product + grad[:, at : at + 128] * w_ref[:, at : at + 128].astype(F32)
    gain_part = dot(jnp.ones((8, 128), F32), product, ((1,), (1,)), lax.Precision.HIGHEST)
    gain_part = gain_part / gain_ref[...]
    for tile in range(3):
        small_ref[8 * tile : 8 * tile + 8, :] = gain_part[:, 128 * tile : 128 * tile + 128]


def attend_back(grads, inputs, fields, mixed, weight, out_weight, scale, groups, gain, name):
    count, part, _ = inputs.shape
    rows = count * part
    return pl.pallas_call(
        attend_back_kernel,
        out_shape=(shape((count, part, C)), shape((12, C, 128)), shape((32, 128), F32)),
        in_specs=vmem(6) + [pl.BlockSpec(memory_space=pltpu.SMEM)] + vmem(3),
        out_specs=tuple(vmem(3)),
        scratch_shapes=[pltpu.VMEM((rows, rows), F32), pltpu.VMEM((rows, 3 * C), BF16)],
        name=name,
    )(grads, inputs, fields, mixed, weight, out_weight, scale, groups[:, None], groups[None, :], gain)


def middle_kernel(tok_ref, dep_ref, tim_ref, pd_ref, pt_ref, out_ref):
    dep = dep_ref[...].astype(F32).reshape(384, C).astype(BF16)
    tim = tim_ref[...].astype(F32).reshape(320, C).astype(BF16)
    total = tok_ref[...].astype(F32) + dot(pd_ref[...], dep, ((0,), (0,)))
    out_ref[...] = (total + dot(pt_ref[...], tim, ((0,), (0,)))).astype(BF16)


def middle_of(tokens, depth, time, pd, pt):
    return pl.pallas_call(
        middle_kernel,
        out_shape=shape((ROWS, C)),
        in_specs=vmem(5),
        out_specs=vmem(1)[0],
        name="middle",
    )(tokens, depth, time, pd, pt)


def down_one(values, first):
    return jnp.where(first, 0.0, pltpu.roll(values, 1, 0))


def up_one(values, last):
    return jnp.where(last, 0.0, pltpu.roll(values, PW - 1, 0))


def act_pair(values):
    square = values * values
    inner = 0.7978845608 * values * (1.0 + 0.044715 * square)
    tanh = jnp.tanh(inner)
    half = 0.5 * (1.0 + tanh)
    slope = 0.7978845608 * (1.0 + 3.0 * 0.044715 * square)
    return values * half, half + 0.5 * values * (1.0 - tanh * tanh) * slope


def feed_kernel(
    low_ref, mid_ref, high_ref, og_low_ref, og_ref, og_high_ref, gain_ref, up_ref, kern_ref, down_ref,
    pd_ref, pt_ref,
    block_ref, mgrad_ref, bdep_ref, btim_ref, weights_ref, kgrad_ref, small_ref,
    norm_ref, og4_ref, hid_ref, fgr_ref, act_ref, hgr_ref, ag_ref, block_acc, back_acc, prod_acc,
):
    step = pl.program_id(0)

    @pl.when(step == 0)
    def _():
        for at, ref in ((0, low_ref), (ROWS, mid_ref), (2 * ROWS, high_ref)):
            scaled, _ = norm_parts(ref[...].astype(F32))
            norm_ref[at : at + ROWS, :] = (scaled * gain_ref[...]).astype(BF16)
        og4_ref[0:CELLS, :] = og_low_ref[...]
        og4_ref[CELLS : CELLS + ROWS, :] = og_ref[...]
        og4_ref[CELLS + ROWS : 2 * ROWS, :] = og_high_ref[...]
        hid_ref[...] = jnp.zeros(hid_ref.shape, F32)
        fgr_ref[...] = jnp.zeros(fgr_ref.shape, F32)
        block_acc[...] = jnp.zeros(block_acc.shape, F32)
        back_acc[...] = jnp.zeros(back_acc.shape, F32)
        prod_acc[...] = jnp.zeros(prod_acc.shape, F32)

    place = lax.broadcasted_iota(jnp.int32, (PW, 128), 0)
    first, last = place == 0, place == PW - 1
    hidden = dot(norm_ref[...], up_ref[...]).astype(BF16).astype(F32)
    ag_ref[...] = dot(og4_ref[...], down_ref[...], ((1,), (1,)))
    for lt in range(2):
        for piece in range(6):
            hid_ref[lt, piece * PAD + PW : piece * PAD + PW + CELLS, :] = hidden[
                piece * CELLS : (piece + 1) * CELLS, 128 * lt : 128 * lt + 128
            ]

    for lt in range(2):
        lanes = slice(128 * lt, 128 * lt + 128)

        def forward(piece, _, lt=lt, lanes=lanes):
            for i in range(6):
                acc = [None] * 3
                for a in range(3):
                    for b in range(3):
                        start = pl.multiple_of((piece + a) * PAD + PW * (i + b), 8)
                        window = hid_ref[lt, pl.ds(start, PW), :]
                        for e in range(3):
                            k = 9 * a + 3 * b + e
                            term = kern_ref[k : k + 1, lanes] * window
                            acc[e] = term if acc[e] is None else acc[e] + term
                filtered = acc[1] + down_one(acc[0], first) + up_one(acc[2], last)
                value, slope = act_pair(filtered)
                at = pl.multiple_of(piece * CELLS + PW * i, 8)
                grad = (ag_ref[pl.ds(at, PW), lanes] * slope).astype(BF16).astype(F32)
                fgr_ref[lt, pl.ds(pl.multiple_of(piece * PAD + PW * (i + 1), 8), PW), :] = grad
                act_ref[pl.ds(at, PW), lanes] = value
            return 0

        lax.fori_loop(0, 4, forward, 0)

        def backward(piece, sums, lt=lt, lanes=lanes):
            sums = list(sums)
            for i in range(6):
                acc = [None] * 3
                for a in range(3):
                    for b in range(3):
                        start = pl.multiple_of((piece + 2 - a) * PAD + PW * (i + 2 - b), 8)
                        window = fgr_ref[lt, pl.ds(start, PW), :]
                        for e in range(3):
                            k = 9 * a + 3 * b + e
                            term = kern_ref[k : k + 1, lanes] * window
                            acc[e] = term if acc[e] is None else acc[e] + term
                total = acc[1] + up_one(acc[0], last) + down_one(acc[2], first)
                hgr_ref[pl.ds(pl.multiple_of(piece * CELLS + PW * i, 8), PW), lanes] = total
            return tuple(sums)

        lax.fori_loop(0, 2, backward, ())

        for a in range(3):

            def products(piece, sums, a=a, lt=lt):
                sums = list(sums)
                for i in range(6):
                    own = pl.multiple_of((piece + 1) * PAD + PW * (i + 1), 8)
                    grad = fgr_ref[lt, pl.ds(own, PW), :]
                    shifted = (up_one(grad, last), grad, down_one(grad, first))
                    for b in range(3):
                        start = pl.multiple_of((piece + 1 + a) * PAD + PW * (i + b), 8)
                        window = hid_ref[lt, pl.ds(start, PW), :]
                        for e in range(3):
                            term = window * shifted[e]
                            k = 3 * b + e
                            sums[k] = sums[k] + (term[0:8] + term[8:16] + term[16:24])
                return tuple(sums)

            sums = lax.fori_loop(0, 2, products, tuple(jnp.zeros((8, 128), F32) for _ in range(9)))
            for k in range(9):
                row = 32 * lt + 9 * a + k
                kgrad_ref[0, row : row + 1, :] = jnp.sum(sums[k], axis=0, keepdims=True)
        kgrad_ref[0, 32 * lt + 27 : 32 * lt + 32, :] = jnp.zeros((5, 128), F32)

    active = act_ref[CELLS : CELLS + ROWS, :].astype(BF16)
    block_acc[...] += dot(active, down_ref[...])
    down_grad = dot(active, og_ref[...], ((0,), (0,)))
    hidden_grad = hgr_ref[...].astype(BF16)
    up_grad = dot(norm_ref[ROWS : 2 * ROWS, :], hidden_grad, ((0,), (0,)))
    back_acc[...] += dot(hidden_grad, up_ref[...], ((1,), (1,)))
    product = up_grad * up_ref[...].astype(F32)
    prod_acc[...] += product[:, :128] + product[:, 128:]
    for tile in range(2):
        weights_ref[0, C * tile : C * tile + C, :] = up_grad[:, 128 * tile : 128 * tile + 128].astype(BF16)
    for tile in range(3):
        at = 2 * C + BLOCK * tile
        weights_ref[0, at : at + BLOCK, :] = down_grad[:, 128 * tile : 128 * tile + 128].astype(BF16)

    @pl.when(step == STEPS - 1)
    def _():
        wide = mid_ref[...].astype(F32)
        block_ref[...] = (wide + block_acc[...]).astype(BF16)
        scaled, inverse = norm_parts(wide)
        back = norm_back(scaled, inverse, back_acc[...] * gain_ref[...])
        middle_grad = og_ref[...].astype(F32) + back
        mgrad_ref[...] = middle_grad
        short = middle_grad.astype(BF16)
        bdep_ref[...] = dot(pd_ref[...], short).reshape(16, 24, C).astype(BF16)
        btim_ref[...] = dot(pt_ref[...], short).reshape(8, 40, C).astype(BF16)
        part = dot(jnp.ones((8, 128), F32), prod_acc[...], ((1,), (1,)), lax.Precision.HIGHEST)
        part = part / gain_ref[...]
        for tile in range(3):
            small_ref[8 * tile : 8 * tile + 8, :] = part[:, 128 * tile : 128 * tile + 128]
        small_ref[24:32, :] = jnp.zeros((8, 128), F32)


def feed_forward(low, mid, high, og_low, og, og_high, gain, up, kern, down, pd, pt):
    def whole(*dims):
        return pl.BlockSpec(dims, lambda s: (0,) * len(dims))

    return pl.pallas_call(
        feed_kernel,
        grid=(STEPS,),
        out_shape=(
            shape((ROWS, C)),
            shape((ROWS, C), F32),
            shape((16, 24, C)),
            shape((8, 40, C)),
            shape((STEPS, 1536, 128)),
            shape((STEPS, 64, 128), F32),
            shape((32, 128), F32),
        ),
        in_specs=[
            whole(ROWS, C),
            whole(ROWS, C),
            whole(ROWS, C),
            whole(CELLS, C),
            whole(ROWS, C),
            whole(CELLS, C),
            whole(1, C),
            pl.BlockSpec((C, BLOCK), lambda s: (0, s)),
            pl.BlockSpec((27, BLOCK), lambda s: (0, s)),
            pl.BlockSpec((BLOCK, C), lambda s: (s, 0)),
            whole(384, ROWS),
            whole(320, ROWS),
        ],
        out_specs=(
            whole(ROWS, C),
            whole(ROWS, C),
            whole(16, 24, C),
            whole(8, 40, C),
            pl.BlockSpec((1, 1536, 128), lambda s: (s, 0, 0)),
            pl.BlockSpec((1, 64, 128), lambda s: (s, 0, 0)),
            whole(32, 128),
        ),
        scratch_shapes=[
            pltpu.VMEM((3 * ROWS, C), BF16),
            pltpu.VMEM((2 * ROWS, C), BF16),
            pltpu.VMEM((2, 6 * PAD, 128), F32),
            pltpu.VMEM((2, 4 * PAD, 128), F32),
            pltpu.VMEM((2 * ROWS, BLOCK), F32),
            pltpu.VMEM((ROWS, BLOCK), F32),
            pltpu.VMEM((2 * ROWS, BLOCK), F32),
            pltpu.VMEM((ROWS, C), F32),
            pltpu.VMEM((ROWS, C), F32),
            pltpu.VMEM((C, 128), F32),
        ],
        name="feed_forward",
    )(low, mid, high, og_low, og, og_high, gain, up, kern, down, pd, pt)


def last_kernel(tok_ref, dep_ref, tim_ref, pd_ref, pt_ref, gain_ref, mgrad_ref, out_ref):
    dep = dep_ref[...].astype(F32).reshape(384, C).astype(BF16)
    tim = tim_ref[...].astype(F32).reshape(320, C).astype(BF16)
    back = dot(pd_ref[...], dep, ((0,), (0,))) + dot(pt_ref[...], tim, ((0,), (0,)))
    scaled, inverse = norm_parts(tok_ref[...].astype(F32))
    out_ref[...] = (mgrad_ref[...] + norm_back(scaled, inverse, back * gain_ref[...])).astype(BF16)


def last_norm(tokens, depth, time, pd, pt, gain, mgrad):
    return pl.pallas_call(
        last_kernel,
        out_shape=shape((ROWS, C)),
        in_specs=vmem(7),
        out_specs=vmem(1)[0],
        name="last_norm",
    )(tokens, depth, time, pd, pt, gain, mgrad)


FFN = 4608
ATT = 2304
TOTAL = COPIES * CHUNK


def pair_kernel(core_ref, f0, f1, d0, d1, t0, t1, k0, k1, s0, s1, out_ref):
    at = 0
    for one, two in ((f0, f1), (d0, d1), (t0, t1), (k0, k1)):
        size = one.shape[1]
        out_ref[at : at + size, :] = (one[0].astype(F32) + two[...].astype(F32)).astype(BF16)
        at += size
    size = s0.shape[0]
    out_ref[at : at + size, :] = (s0[...] + s1[...].astype(F32)).astype(BF16)
    out_ref[at + size :, :] = jnp.zeros((TOTAL - at - size, 128), BF16)


def pair_sum(core, pairs):
    specs, args = [], []
    for mine, theirs in pairs[:-1]:
        rows = mine.shape[1]
        specs.append(pl.BlockSpec((1, rows, 128), lambda i, c: (c[0], 0, 0)))
        specs.append(pl.BlockSpec((rows, 128), lambda i, c: (0, 0)))
        args += [mine, theirs]
    for array in pairs[-1]:
        specs.append(pl.BlockSpec(array.shape, lambda i, c: (0, 0)))
        args.append(array)
    return pl.pallas_call(
        pair_kernel,
        out_shape=shape((TOTAL, 128)),
        grid_spec=pltpu.PrefetchScalarGridSpec(
            num_scalar_prefetch=1,
            grid=(1,),
            in_specs=specs,
            out_specs=pl.BlockSpec((TOTAL, 128), lambda i, c: (0, 0)),
        ),
        name="pair_sum",
    )(core, *args)


def chip_kernel(factor, in_ref, out_ref):
    total = in_ref[0].astype(F32)
    for source in range(1, COPIES):
        total = total + in_ref[source].astype(F32)
    total = (total * factor).astype(BF16)
    for target in range(COPIES):
        out_ref[target] = total


def chip_sum(received, factor):
    return pl.pallas_call(
        functools.partial(chip_kernel, factor),
        out_shape=shape((COPIES, CHUNK, 128)),
        in_specs=vmem(1),
        out_specs=vmem(1)[0],
        name="chip_sum",
    )(received)


def unpack_kernel(core_ref, own_ref, other_ref, dq_ref, do_ref, tq_ref, to_ref, up_ref, kg_ref, dn_ref, small_ref):
    zero = core_ref[0] == 0

    def part(half, at, rows):
        own = own_ref[at : at + rows, :].astype(F32)
        other = other_ref[at : at + rows, :].astype(F32)
        return jnp.where(zero, own, other) if half == 0 else jnp.where(zero, other, own)

    for step in range(STEPS):
        half, at = step // 3, 1536 * (step % 3)
        for tile in range(2):
            lanes = slice(BLOCK * step + 128 * tile, BLOCK * step + 128 * tile + 128)
            up_ref[:, lanes] = part(half, at + C * tile, C)
            kg_ref[:, lanes] = part(half, FFN + 2 * ATT + 64 * (step % 3) + 32 * tile, 32)[:27]
        for tile in range(3):
            lanes = slice(128 * tile, 128 * tile + 128)
            dn_ref[BLOCK * step : BLOCK * step + BLOCK, lanes] = part(half, at + 2 * C + BLOCK * tile, BLOCK)
    for base, q_ref, o_ref in ((FFN, dq_ref, do_ref), (FFN + ATT, tq_ref, to_ref)):
        for tile in range(12):
            half, at = tile // 6, base + C * (tile % 6)
            if tile < 9:
                q_ref[:, 128 * tile : 128 * tile + 128] = part(half, at, C)
            else:
                o_ref[:, 128 * (tile - 9) : 128 * (tile - 9) + 128] = part(half, at, C)
    small_ref[...] = part(0, FFN + 2 * ATT + 192, 96)


def unpack(core, own, other):
    return pl.pallas_call(
        unpack_kernel,
        out_shape=(
            shape((C, 3 * C), F32),
            shape((C, C), F32),
            shape((C, 3 * C), F32),
            shape((C, C), F32),
            shape((C, HID), F32),
            shape((27, HID), F32),
            shape((HID, C), F32),
            shape((96, 128), F32),
        ),
        in_specs=[pl.BlockSpec(memory_space=pltpu.SMEM)] + vmem(2),
        out_specs=tuple(vmem(8)),
        name="unpack",
    )(core, own, other)


def local(
    tokens, out_grad, first_gain, depth_qkv, depth_out, time_qkv, time_out, second_gain, up_weight,
    spatial_kernel, down_weight, depth_scale, time_scale,
):
    pd = jnp.asarray(spread_depth(), BF16)
    pt = jnp.asarray(spread_time(), BF16)
    gd = jnp.asarray(groups_depth())
    gt = jnp.asarray(groups_time())
    core_index = lax.axis_index("core").astype(jnp.int32)
    core = core_index.reshape(1)
    block_shape = tokens.shape
    flat = tokens.reshape(ROWS, C)
    og = out_grad.reshape(ROWS, C)
    gain_one = first_gain.reshape(1, C)
    gain_two = second_gain.reshape(1, C)
    count = lax.axis_size(DEV)
    ahead = [(i, i + 1) for i in range(count - 1)]
    behind = [(i + 1, i) for i in range(count - 1)]
    swap = [(0, 1), (1, 0)]

    def exchange(values, axes):
        return lax.all_to_all(values, axes, split_axis=0, concat_axis=0, tiled=True)

    dep, tim = first_norm(flat, gain_one, pd, pt)
    dep = exchange(dep, DEV)
    tim = exchange(tim, TA)
    og_low = lax.ppermute(og[CELLS:], DEV, ahead)
    og_high = lax.ppermute(og[:CELLS], DEV, behind)
    dep_out, dep_fields, dep_mixed = attend(dep, depth_qkv, depth_out, depth_scale, gd, "depth_attend")
    dep_back = exchange(dep_out, DEV)
    tim_out, tim_fields, tim_mixed = attend(tim, time_qkv, time_out, time_scale, gt, "time_attend")
    tim_back = exchange(tim_out, TA)
    mid = middle_of(flat, dep_back, tim_back, pd, pt)
    low = lax.ppermute(mid, DEV, ahead)
    high = lax.ppermute(mid, DEV, behind)
    block_out, mgrad, bdep, btim, ffn_g, kern_g, small_g = feed_forward(
        low, mid, high, og_low, og, og_high, gain_two, up_weight, spatial_kernel.reshape(27, HID),
        down_weight, pd, pt,
    )
    bdep = exchange(bdep, DEV)
    btim = exchange(btim, TA)
    dep_first, dep_g, dep_small = attend_back(
        bdep, dep, dep_fields, dep_mixed, depth_qkv, depth_out, depth_scale, gd, gain_one, "depth_back"
    )
    dep_first = exchange(dep_first, DEV)
    tim_first, tim_g, tim_small = attend_back(
        btim, tim, tim_fields, tim_mixed, time_qkv, time_out, time_scale, gt, gain_one, "time_back"
    )
    tim_first = exchange(tim_first, TA)
    input_grad = last_norm(flat, dep_first, tim_first, pd, pt, gain_one, mgrad)

    def swapped(halves):
        return lax.ppermute(lax.dynamic_index_in_dim(halves, 1 - core_index, 0, keepdims=False), "core", swap)

    halves = [
        ffn_g.reshape(2, FFN, 128),
        dep_g.reshape(2, ATT, 128),
        tim_g.reshape(2, ATT, 128),
        kern_g.reshape(2, 192, 128),
    ]
    pairs = [(half, swapped(half)) for half in halves]
    small = jnp.concatenate([small_g, dep_small, tim_small], axis=0)
    pairs.append((small, lax.ppermute(small, "core", swap)))
    stack = pair_sum(core, pairs)
    received = exchange(stack.reshape(COPIES, CHUNK, 128), CHIPS)
    factor = 1.0 / math.sqrt(ROWS * count * lax.axis_size(TA))
    own = exchange(chip_sum(received, factor), CHIPS).reshape(TOTAL, 128)
    other = lax.ppermute(own, "core", swap)
    dq, do, tq, to, up_g, kern_sum, down_g, small = unpack(core, own, other)
    small = small.reshape(12, 8, 128)
    second_gain_grad = small[0:3, 0].reshape(C)
    first_gain_grad = (small[4:7, 0] + small[8:11, 0]).reshape(C)
    depth_scale_grad = small[7, 0:3, ::64].reshape(6)
    time_scale_grad = small[11, 0:3, ::64].reshape(6)
    return (
        block_out.reshape(block_shape),
        input_grad.reshape(block_shape),
        dq,
        do,
        tq,
        to,
        up_g,
        kern_sum.reshape(3, 3, 3, HID),
        down_g,
        first_gain_grad,
        second_gain_grad,
        depth_scale_grad,
        time_scale_grad,
    )


def solution(mesh):
    fine = Mesh(mesh.devices.reshape(4, 2, 2, 2, 4), ("y", "xh", "core", "xl", "z"))
    split = P(TA, DEV, None, None)
    return jax.shard_map(
        local,
        mesh=fine,
        in_specs=(split, split) + (P(),) * 11,
        out_specs=(split, split) + (P(),) * 11,
        check_vma=False,
    )
```

```python
import functools
import math

import jax
import jax.numpy as jnp
import numpy as np
from jax import lax
from jax.experimental import pallas as pl
from jax.experimental.pallas import tpu as pltpu
from jax.sharding import Mesh
from jax.sharding import PartitionSpec as P


C = 384
HID = 1536
PW = 24
CELLS = 144
ROWS = 288
BLOCK = 256
STEPS = HID // BLOCK
PAD = 192
DEV = ("y", "xh", "core")
TA = ("xl", "z")
CHIPS = ("y", "xh", "xl", "z")
COPIES = 64
CHUNK = 80
F32 = jnp.float32
BF16 = jnp.bfloat16
EPS = 1e-5


def spread_depth():
    table = np.zeros((16, 24, ROWS), np.float32)
    for owner in range(16):
        for k in range(18):
            table[owner, k, (k // 9) * CELLS + 9 * owner + k % 9] = 1
    return table.reshape(384, ROWS)


def spread_time():
    table = np.zeros((8, 40, ROWS), np.float32)
    for owner in range(8):
        for k in range(36):
            table[owner, k, (k // 18) * CELLS + 18 * owner + k % 18] = 1
    return table.reshape(320, ROWS)


def groups_depth():
    k = np.arange(384) % 24
    return np.where(k < 18, k % 9, k - 9).astype(np.int32)


def groups_time():
    return (np.arange(320) % 40).astype(np.int32)


def dot(left, right, dims=((1,), (0,)), precision=None):
    return lax.dot_general(
        left, right, (dims, ((), ())), preferred_element_type=F32, precision=precision
    )


def norm_parts(values):
    centered = values - jnp.mean(values, axis=-1, keepdims=True)
    inverse = lax.rsqrt(jnp.mean(centered * centered, axis=-1, keepdims=True) + EPS)
    return centered * inverse, inverse


def norm_back(scaled, inverse, grads):
    mean = jnp.mean(grads, axis=-1, keepdims=True)
    along = jnp.mean(grads * scaled, axis=-1, keepdims=True)
    return (grads - mean - scaled * along) * inverse


def vmem(count):
    return [pl.BlockSpec(memory_space=pltpu.VMEM)] * count


SMEM = [pl.BlockSpec(memory_space=pltpu.SMEM)]


def shape(dims, kind=BF16):
    return jax.ShapeDtypeStruct(dims, kind)


def deal(values, turn, mask, part_refs, hold_ref):
    count = len(part_refs)
    hold_ref[...] = values.reshape(count, values.shape[0] // count, C)
    for step, ref in enumerate(part_refs):
        ref[...] = hold_ref[(turn + step) & mask].astype(BF16)


def row_of(ref):
    return ref[...].reshape(1, ref.shape[0])


def first_kernel(tok_ref, gain_ref, pd_ref, pt_ref, dep_ref, tim_ref):
    scaled, _ = norm_parts(tok_ref[...].astype(F32))
    normed = (scaled * row_of(gain_ref)).astype(BF16)
    dep_ref[...] = dot(pd_ref[...], normed).reshape(16, 24, C).astype(BF16)
    tim_ref[...] = dot(pt_ref[...], normed).reshape(8, 40, C).astype(BF16)


def first_norm(tokens, gain, pd, pt):
    return pl.pallas_call(
        first_kernel,
        out_shape=(shape((16, 24, C)), shape((8, 40, C))),
        in_specs=vmem(4),
        out_specs=tuple(vmem(2)),
        name="first_norm",
    )(tokens, gain, pd, pt)


ATT = 2304


def lane_is_low():
    return lax.broadcasted_iota(jnp.int32, (1, 128), 1) < 64


def head_ones():
    row = lax.broadcasted_iota(jnp.int32, (128, 128), 0) < 64
    col = lax.broadcasted_iota(jnp.int32, (128, 128), 1) < 64
    return jnp.where(row == col, 1.0, 0.0).astype(BF16)


def head_sum(values, ones):
    high = values.astype(BF16)
    low = (values - high.astype(F32)).astype(BF16)
    return dot(high, ones) + dot(low, ones)


def joined(refs):
    if len(refs) == 1:
        count, part, _ = refs[0].shape
        return refs[0][...].astype(F32).reshape(count * part, C).astype(BF16)
    return jnp.concatenate([ref[...].astype(F32) for ref in refs], axis=0).astype(BF16)


def dealt(values, refs):
    if len(refs) == 1:
        refs[0][...] = values.reshape(refs[0].shape).astype(BF16)
        return
    part = values.shape[0] // len(refs)
    for step, ref in enumerate(refs):
        ref[...] = values[part * step : part * step + part].astype(BF16)


def attend_kernel(count, *refs):
    in_refs, refs = refs[:count], refs[count:]
    w_ref, wo_ref, scale_ref, gr_ref, gc_ref = refs[:5]
    out_refs, (fields_ref, mixed_ref, same_ref) = refs[5 : 5 + count], refs[5 + count :]
    rowed = joined(in_refs)
    rows = rowed.shape[0]
    fields_ref[...] = dot(rowed, w_ref[...]).astype(BF16)
    same_ref[...] = jnp.where(gr_ref[...] == gc_ref[...], 1.0, 0.0)
    ones = head_ones()
    low = lane_is_low()
    side = jnp.ones((rows, 128), BF16)

    def one_pair(pair, _):
        at = pl.multiple_of(128 * pair, 128)
        query = fields_ref[:, pl.ds(at, 128)].astype(F32)
        keyed = fields_ref[:, pl.ds(C + at, 128)].astype(F32)
        valued = fields_ref[:, pl.ds(2 * C + at, 128)]
        query = query * lax.rsqrt(head_sum(query * query, ones) + 1e-6)
        keyed = (keyed * lax.rsqrt(head_sum(keyed * keyed, ones) + 1e-6)).astype(BF16)
        query = query * jnp.where(low, scale_ref[2 * pair], scale_ref[2 * pair + 1])
        both = jnp.concatenate([valued, side], axis=1)
        results = []
        for half in range(2):
            mine = low if half == 0 else jnp.logical_not(low)
            scores = dot(jnp.where(mine, query, 0.0).astype(BF16), keyed, ((1,), (1,)))
            weights = (jnp.exp(scores) * same_ref[...]).astype(BF16)
            sums = dot(weights, both)
            results.append(sums[:, :128] / sums[:, 128:])
        mixed_ref[:, pl.ds(at, 128)] = jnp.where(low, results[0], results[1]).astype(BF16)
        return 0

    lax.fori_loop(0, 3, one_pair, 0)
    dealt(dot(mixed_ref[...], wo_ref[...]), out_refs)


def attend(inputs, weight, out_weight, scale, groups):
    count, rows = len(inputs), groups.shape[0]
    outs = pl.pallas_call(
        functools.partial(attend_kernel, count),
        out_shape=tuple(shape(x.shape) for x in inputs) + (shape((rows, 3 * C)), shape((rows, C))),
        in_specs=vmem(count + 2) + SMEM + vmem(2),
        out_specs=tuple(vmem(count + 2)),
        scratch_shapes=[pltpu.VMEM((rows, rows), F32)],
    )(*inputs, weight, out_weight, scale, groups[:, None], groups[None, :])
    return outs[:count], outs[count], outs[count + 1]


def put_tile(ref, tile, values):
    for half in range(2):
        ref[half, 192 * tile : 192 * tile + 192, :] = values[192 * half : 192 * half + 192].astype(BF16)


def attend_back_kernel(count, out_count, *refs):
    grad_refs, in_refs, refs = refs[:count], refs[count : 2 * count], refs[2 * count :]
    me_ref, fields_ref, mixed_ref, w_ref, wo_ref, scale_ref, gr_ref, gc_ref, gain_ref = refs[:9]
    out_refs, refs = refs[9 : 9 + out_count], refs[9 + out_count :]
    weights_ref, small_ref, same_ref, fg_ref, cot_ref = refs[:5]
    grads = joined(grad_refs)
    rows = grads.shape[0]
    same_ref[...] = jnp.where(gr_ref[...] == gc_ref[...], 1.0, 0.0)
    out_grad = dot(mixed_ref[...], grads, ((0,), (0,)))
    for tile in range(3):
        put_tile(weights_ref, 9 + tile, out_grad[:, 128 * tile : 128 * tile + 128])
    cot_ref[...] = dot(grads, wo_ref[...], ((1,), (1,))).astype(BF16)
    ones = head_ones()
    low = lane_is_low()
    side = jnp.ones((rows, 128), BF16)
    small_ref[24:32, :] = jnp.zeros((8, 128), F32)

    def one_pair(pair, _):
        at = pl.multiple_of(128 * pair, 128)
        query = fields_ref[:, pl.ds(at, 128)].astype(F32)
        keyed = fields_ref[:, pl.ds(C + at, 128)].astype(F32)
        valued = fields_ref[:, pl.ds(2 * C + at, 128)]
        query_inv = lax.rsqrt(head_sum(query * query, ones) + 1e-6)
        keyed_inv = lax.rsqrt(head_sum(keyed * keyed, ones) + 1e-6)
        query = query * query_inv
        keyed = keyed * keyed_inv
        scale = jnp.where(low, scale_ref[2 * pair], scale_ref[2 * pair + 1])
        scaled = query * scale
        keyed_short = keyed.astype(BF16)
        cot = cot_ref[:, pl.ds(at, 128)]
        delta = head_sum(cot.astype(F32) * mixed_ref[:, pl.ds(at, 128)].astype(F32), ones)
        query_grad = jnp.zeros((rows, 128), F32)
        keyed_grad = jnp.zeros((rows, 128), F32)
        value_grad = jnp.zeros((rows, 128), F32)
        for half in range(2):
            mine = low if half == 0 else jnp.logical_not(low)
            lane = 64 * half
            mine_query = jnp.where(mine, scaled, 0.0).astype(BF16)
            mine_cot = jnp.where(mine, cot.astype(F32), 0.0).astype(BF16)
            mine_keyed = jnp.where(mine, keyed, 0.0).astype(BF16)
            scores = dot(mine_query, keyed_short, ((1,), (1,)))
            weights = jnp.exp(scores) * same_ref[...]
            total = dot(weights.astype(BF16), side)
            weights = weights * (1.0 / total)[:, :1]
            weights_grad = dot(mine_cot, valued, ((1,), (1,)))
            scores_grad = (weights * (weights_grad - delta[:, lane : lane + 1])).astype(BF16)
            value_grad = value_grad + dot(weights.astype(BF16), mine_cot, ((0,), (0,)))
            query_grad = query_grad + dot(scores_grad, mine_keyed)
            keyed_grad = keyed_grad + dot(scores_grad, mine_query, ((0,), (0,)))
        along = jnp.sum(query_grad * query, axis=0, keepdims=True)
        small_ref[pl.ds(24 + pair, 1), :] = head_sum(jnp.broadcast_to(along, (8, 128)), ones)[:1]
        query_grad = query_grad * scale
        query_grad = (query_grad - query * head_sum(query * query_grad, ones)) * query_inv
        keyed_grad = (keyed_grad - keyed * head_sum(keyed * keyed_grad, ones)) * keyed_inv
        fg_ref[:, pl.ds(at, 128)] = query_grad.astype(BF16)
        fg_ref[:, pl.ds(C + at, 128)] = keyed_grad.astype(BF16)
        fg_ref[:, pl.ds(2 * C + at, 128)] = value_grad.astype(BF16)
        return 0

    lax.fori_loop(0, 3, one_pair, 0)
    back = dot(fg_ref[...], w_ref[...], ((1,), (1,)))
    if out_count == 16:
        deal(back, me_ref[2], 15, out_refs, refs[5])
    else:
        dealt(back, out_refs)
    grad = dot(joined(in_refs), fg_ref[...], ((0,), (0,)))
    product = jnp.zeros((C, 128), F32)
    for tile in range(9):
        at = 128 * tile
        put_tile(weights_ref, tile, grad[:, at : at + 128])
        product = product + grad[:, at : at + 128] * w_ref[:, at : at + 128].astype(F32)
    gain_part = dot(jnp.ones((8, 128), F32), product, ((1,), (1,)), lax.Precision.HIGHEST)
    gain_part = gain_part / row_of(gain_ref)
    for tile in range(3):
        small_ref[8 * tile : 8 * tile + 8, :] = gain_part[:, 128 * tile : 128 * tile + 128]
    for half in range(2):
        weights_ref[half, ATT:, :] = small_ref[...].astype(BF16)


def attend_back(me, grads, inputs, fields, mixed, weight, out_weight, scale, groups, gain, deals):
    count, rows = len(inputs), groups.shape[0]
    part = rows // 16
    scratch = [pltpu.VMEM((32, 128), F32), pltpu.VMEM((rows, rows), F32), pltpu.VMEM((rows, 3 * C), BF16)]
    scratch.append(pltpu.VMEM((rows, C), BF16))
    if deals == 16:
        scratch.append(pltpu.VMEM((16, part, C), F32))
    outs = pl.pallas_call(
        functools.partial(attend_back_kernel, count, deals),
        out_shape=((shape((part, C)),) * 16 if deals == 16 else (shape(inputs[0].shape),))
        + (shape((2, ATT + 32, 128)),),
        in_specs=vmem(2 * count) + SMEM + vmem(4) + SMEM + vmem(3),
        out_specs=tuple(vmem(deals + 1)),
        scratch_shapes=scratch,
    )(*grads, *inputs, me, fields, mixed, weight, out_weight, scale, groups[:, None], groups[None, :], gain)
    return outs[:deals], outs[deals]


def middle_kernel(tok_ref, pd_ref, pt_ref, dep_ref, tim_ref, out_ref):
    total = tok_ref[...].astype(F32) + dot(pd_ref[...], joined([dep_ref]), ((0,), (0,)))
    out_ref[...] = (total + dot(pt_ref[...], joined([tim_ref]), ((0,), (0,)))).astype(BF16)


def middle_of(tokens, depth, time, pd, pt):
    return pl.pallas_call(
        middle_kernel,
        out_shape=shape((ROWS, C)),
        in_specs=vmem(5),
        out_specs=vmem(1)[0],
        name="middle",
    )(tokens, pd, pt, depth, time)


STRIDE = 1600
FFN = 3 * STRIDE


def down_one(values, first):
    return jnp.where(first, 0.0, pltpu.roll(values, 1, 0))


def up_one(values, last):
    return jnp.where(last, 0.0, pltpu.roll(values, PW - 1, 0))


def act_pair(values):
    square = values * values
    inner = 0.7978845608 * values * (1.0 + 0.044715 * square)
    tanh = jnp.tanh(inner)
    half = 0.5 * (1.0 + tanh)
    slope = 0.7978845608 * (1.0 + 3.0 * 0.044715 * square)
    return values * half, half + 0.5 * values * (1.0 - tanh * tanh) * slope


def feed_kernel(
    low_ref, mid_ref, high_ref, og_low_ref, og_ref, og_high_ref, gain_ref, up_ref, kern_ref, down_ref,
    pd_ref, pt_ref, block_ref, mgrad_ref, weights_ref, bdep_ref, btim_ref,
    norm_ref, og4_ref, hid_ref, fgr_ref, act_ref, hgr_ref, ag_ref, block_acc, back_acc, prod_acc, kgrad_ref,
):
    step = pl.program_id(0)

    @pl.when(step == 0)
    def _():
        for at, ref in ((0, low_ref), (ROWS, mid_ref), (2 * ROWS, high_ref)):
            scaled, _ = norm_parts(ref[...].astype(F32))
            norm_ref[at : at + ROWS, :] = (scaled * row_of(gain_ref)).astype(BF16)
        og4_ref[0:CELLS, :] = og_low_ref[...]
        og4_ref[CELLS : CELLS + ROWS, :] = og_ref[...]
        og4_ref[CELLS + ROWS : 2 * ROWS, :] = og_high_ref[...]
        hid_ref[...] = jnp.zeros(hid_ref.shape, F32)
        fgr_ref[...] = jnp.zeros(fgr_ref.shape, F32)
        block_acc[...] = jnp.zeros(block_acc.shape, F32)
        back_acc[...] = jnp.zeros(back_acc.shape, F32)
        prod_acc[...] = jnp.zeros(prod_acc.shape, F32)

    place = lax.broadcasted_iota(jnp.int32, (PW, 128), 0)
    first, last = place == 0, place == PW - 1
    hidden = dot(norm_ref[...], up_ref[...]).astype(BF16).astype(F32)
    ag_ref[...] = dot(og4_ref[...], down_ref[...], ((1,), (1,)))
    for lt in range(2):
        for piece in range(6):
            hid_ref[lt, piece * PAD + PW : piece * PAD + PW + CELLS, :] = hidden[
                piece * CELLS : (piece + 1) * CELLS, 128 * lt : 128 * lt + 128
            ]

    for lt in range(2):
        lanes = slice(128 * lt, 128 * lt + 128)

        def forward(piece, _, lt=lt, lanes=lanes):
            for i in range(6):
                acc = [None] * 3
                for a in range(3):
                    for b in range(3):
                        start = pl.multiple_of((piece + a) * PAD + PW * (i + b), 8)
                        window = hid_ref[lt, pl.ds(start, PW), :]
                        for e in range(3):
                            term = kern_ref[a, b, e : e + 1, lanes] * window
                            acc[e] = term if acc[e] is None else acc[e] + term
                filtered = acc[1] + down_one(acc[0], first) + up_one(acc[2], last)
                value, slope = act_pair(filtered)
                at = pl.multiple_of(piece * CELLS + PW * i, 8)
                grad = (ag_ref[pl.ds(at, PW), lanes] * slope).astype(BF16).astype(F32)
                fgr_ref[lt, pl.ds(pl.multiple_of(piece * PAD + PW * (i + 1), 8), PW), :] = grad
                act_ref[pl.ds(at, PW), lanes] = value
            return 0

        lax.fori_loop(0, 4, forward, 0)

        def backward(piece, sums, lt=lt, lanes=lanes):
            sums = list(sums)
            for i in range(6):
                acc = [None] * 3
                for a in range(3):
                    for b in range(3):
                        start = pl.multiple_of((piece + 2 - a) * PAD + PW * (i + 2 - b), 8)
                        window = fgr_ref[lt, pl.ds(start, PW), :]
                        for e in range(3):
                            term = kern_ref[a, b, e : e + 1, lanes] * window
                            acc[e] = term if acc[e] is None else acc[e] + term
                total = acc[1] + up_one(acc[0], last) + down_one(acc[2], first)
                hgr_ref[pl.ds(pl.multiple_of(piece * CELLS + PW * i, 8), PW), lanes] = total
            return tuple(sums)

        lax.fori_loop(0, 2, backward, ())

        for a in range(3):

            def products(piece, sums, a=a, lt=lt):
                sums = list(sums)
                for i in range(6):
                    own = pl.multiple_of((piece + 1) * PAD + PW * (i + 1), 8)
                    grad = fgr_ref[lt, pl.ds(own, PW), :]
                    shifted = (up_one(grad, last), grad, down_one(grad, first))
                    for b in range(3):
                        start = pl.multiple_of((piece + 1 + a) * PAD + PW * (i + b), 8)
                        window = hid_ref[lt, pl.ds(start, PW), :]
                        for e in range(3):
                            term = window * shifted[e]
                            k = 3 * b + e
                            sums[k] = sums[k] + (term[0:8] + term[8:16] + term[16:24])
                return tuple(sums)

            sums = lax.fori_loop(0, 2, products, tuple(jnp.zeros((8, 128), F32) for _ in range(9)))
            for k in range(9):
                row = 32 * lt + 9 * a + k
                kgrad_ref[row : row + 1, :] = jnp.sum(sums[k], axis=0, keepdims=True)
        kgrad_ref[32 * lt + 27 : 32 * lt + 32, :] = jnp.zeros((5, 128), F32)

    active = act_ref[CELLS : CELLS + ROWS, :].astype(BF16)
    block_acc[...] += dot(active, down_ref[...])
    down_grad = dot(active, og_ref[...], ((0,), (0,)))
    hidden_grad = hgr_ref[...].astype(BF16)
    up_grad = dot(norm_ref[ROWS : 2 * ROWS, :], hidden_grad, ((0,), (0,)))
    back_acc[...] += dot(hidden_grad, up_ref[...], ((1,), (1,)))
    product = up_grad * up_ref[...].astype(F32)
    prod_acc[...] += product[:, :128] + product[:, 128:]
    half = step // 3
    base = pl.multiple_of((step - 3 * half) * STRIDE, 16)
    for tile in range(2):
        weights_ref[half, pl.ds(base + C * tile, C), :] = up_grad[:, 128 * tile : 128 * tile + 128].astype(BF16)
    for tile in range(3):
        at = 2 * C + BLOCK * tile
        weights_ref[half, pl.ds(base + at, BLOCK), :] = down_grad[:, 128 * tile : 128 * tile + 128].astype(BF16)
    weights_ref[half, pl.ds(base + 1536, 64), :] = kgrad_ref[...].astype(BF16)

    @pl.when(step == STEPS - 1)
    def _():
        wide = mid_ref[...].astype(F32)
        block_ref[...] = (wide + block_acc[...]).astype(BF16)
        scaled, inverse = norm_parts(wide)
        back = norm_back(scaled, inverse, back_acc[...] * row_of(gain_ref))
        middle_grad = og_ref[...].astype(F32) + back
        mgrad_ref[...] = middle_grad
        short = middle_grad.astype(BF16)
        bdep_ref[...] = dot(pd_ref[...], short).reshape(16, 24, C).astype(BF16)
        btim_ref[...] = dot(pt_ref[...], short).reshape(8, 40, C).astype(BF16)
        part = dot(jnp.ones((8, 128), F32), prod_acc[...], ((1,), (1,)), lax.Precision.HIGHEST)
        part = part / row_of(gain_ref)
        for tile in range(3):
            kgrad_ref[8 * tile : 8 * tile + 8, :] = part[:, 128 * tile : 128 * tile + 128]
        kgrad_ref[24:32, :] = jnp.zeros((8, 128), F32)
        for side in range(2):
            weights_ref[side, 3 * STRIDE :, :] = kgrad_ref[0:32, :].astype(BF16)


def feed_forward(low, mid, high, og_low, og, og_high, gain, up, kern, down, pd, pt):
    def whole(*dims):
        return pl.BlockSpec(dims, lambda s: (0,) * len(dims))

    return pl.pallas_call(
        feed_kernel,
        grid=(STEPS,),
        out_shape=(
            shape((ROWS, C)),
            shape((ROWS, C), F32),
            shape((2, FFN + 32, 128)),
            shape((16, 24, C)),
            shape((8, 40, C)),
        ),
        in_specs=[
            whole(ROWS, C),
            whole(ROWS, C),
            whole(ROWS, C),
            whole(CELLS, C),
            whole(ROWS, C),
            whole(CELLS, C),
            whole(C),
            pl.BlockSpec((C, BLOCK), lambda s: (0, s)),
            pl.BlockSpec((3, 3, 3, BLOCK), lambda s: (0, 0, 0, s)),
            pl.BlockSpec((BLOCK, C), lambda s: (s, 0)),
            whole(384, ROWS),
            whole(320, ROWS),
        ],
        out_specs=(
            whole(ROWS, C),
            whole(ROWS, C),
            whole(2, FFN + 32, 128),
            whole(16, 24, C),
            whole(8, 40, C),
        ),
        scratch_shapes=[
            pltpu.VMEM((3 * ROWS, C), BF16),
            pltpu.VMEM((2 * ROWS, C), BF16),
            pltpu.VMEM((2, 6 * PAD, 128), F32),
            pltpu.VMEM((2, 4 * PAD, 128), F32),
            pltpu.VMEM((2 * ROWS, BLOCK), F32),
            pltpu.VMEM((ROWS, BLOCK), F32),
            pltpu.VMEM((2 * ROWS, BLOCK), F32),
            pltpu.VMEM((ROWS, C), F32),
            pltpu.VMEM((ROWS, C), F32),
            pltpu.VMEM((C, 128), F32),
            pltpu.VMEM((64, 128), F32),
        ],
        name="feed_forward",
    )(low, mid, high, og_low, og, og_high, gain, up, kern, down, pd, pt)


def last_kernel(me_ref, tok_ref, pd_ref, pt_ref, gain_ref, mgrad_ref, tim_ref, *rest):
    dep_refs, (out_ref, dep_hold) = rest[:16], rest[16:]
    for step, ref in enumerate(dep_refs):
        dep_hold[(me_ref[2] - step) & 15] = ref[...].astype(F32)
    dep = dep_hold[...].reshape(384, C).astype(BF16)
    back = dot(pd_ref[...], dep, ((0,), (0,))) + dot(pt_ref[...], joined([tim_ref]), ((0,), (0,)))
    scaled, inverse = norm_parts(tok_ref[...].astype(F32))
    out_ref[...] = (mgrad_ref[...] + norm_back(scaled, inverse, back * row_of(gain_ref))).astype(BF16)


def last_norm(me, tokens, depth, time, pd, pt, gain, mgrad):
    return pl.pallas_call(
        last_kernel,
        out_shape=shape((ROWS, C)),
        in_specs=SMEM + vmem(22),
        out_specs=vmem(1)[0],
        scratch_shapes=[pltpu.VMEM((16, 24, C), F32)],
        name="last_norm",
    )(me, tokens, pd, pt, gain, mgrad, time, *depth)


STACK = COPIES * CHUNK
DEP = 0
TIM = DEP + ATT + 32


def pair_kernel(me_ref, *refs):
    out_ref, at = refs[-1], 0
    for one, two in zip(refs[0:-1:2], refs[1:-1:2], strict=True):
        size = one.shape[1]
        out_ref[at : at + size, :] = (one[0].astype(F32) + two[0].astype(F32)).astype(BF16)
        at += size
    out_ref[at:, :] = jnp.zeros((STACK - at, 128), BF16)


def swapped(array):
    return lax.ppermute(array, "core", [(0, 1), (1, 0)])


def pair_sum(me, args):
    return pl.pallas_call(
        pair_kernel,
        out_shape=shape((STACK, 128)),
        grid_spec=pltpu.PrefetchScalarGridSpec(
            num_scalar_prefetch=1,
            grid=(1,),
            in_specs=[pl.BlockSpec((1,) + a.shape[1:], lambda i, m: (m[0], 0, 0)) for a in args],
            out_specs=pl.BlockSpec((STACK, 128), lambda i, m: (0, 0)),
        ),
    )(me, *args)


def chip_total(factor, in_ref):
    def add(source, total):
        return total + in_ref[source].astype(F32)

    total = lax.fori_loop(1, COPIES, add, in_ref[0].astype(F32), unroll=3)
    return (total * factor).astype(BF16)


def chip_kernel(factor, in_ref, out_ref):
    out_ref[...] = chip_total(factor, in_ref)


def chip_spread_kernel(factor, in_ref, other_ref, out_ref):
    total = chip_total(factor, in_ref)
    other = other_ref[...]

    def put(target, _):
        out_ref[target, :CHUNK, :] = other
        out_ref[target, CHUNK:, :] = total
        return 0

    lax.fori_loop(0, COPIES, put, 0, unroll=2)


def chip_sum(received, factor):
    return pl.pallas_call(
        functools.partial(chip_kernel, factor),
        out_shape=shape((CHUNK, 128)),
        in_specs=vmem(1),
        out_specs=vmem(1)[0],
        name="chip_sum",
    )(received)


def chip_spread(received, other, factor):
    return pl.pallas_call(
        functools.partial(chip_spread_kernel, factor),
        out_shape=shape((COPIES, 2 * CHUNK, 128)),
        in_specs=vmem(2),
        out_specs=vmem(1)[0],
        name="chip_spread",
    )(received, other)


def unpack_kernel(own, me_ref, in_ref, *refs):
    refs = refs if own else refs[7:]
    dq_ref, do_ref, tq_ref, to_ref, up_ref, kg_ref, dn_ref = refs[:7]
    ffn_ref, att_ref = refs[-2:]

    def split(source, _):
        at = pl.multiple_of(CHUNK * source, 16)
        ffn_ref[pl.ds(at, CHUNK), :] = in_ref[source, :CHUNK, :]
        att_ref[pl.ds(at, CHUNK), :] = in_ref[source, CHUNK:, :]
        return 0

    lax.fori_loop(0, COPIES, split, 0, unroll=2)
    for step in range(3):
        at = STRIDE * step
        for tile in range(2):
            lanes = slice(BLOCK * step + 128 * tile, BLOCK * step + 128 * tile + 128)
            up_ref[:, lanes] = ffn_ref[at + C * tile : at + C * tile + C, :].astype(F32)
            kgrad = ffn_ref[at + 1536 + 32 * tile : at + 1568 + 32 * tile, :].astype(F32)
            for k in range(27):
                kg_ref[k // 9, k // 3 % 3, k % 3 : k % 3 + 1, lanes] = kgrad[k : k + 1]
        for tile in range(3):
            rows = ffn_ref[at + 768 + BLOCK * tile : at + 1024 + BLOCK * tile, :].astype(F32)
            dn_ref[BLOCK * step : BLOCK * step + BLOCK, 128 * tile : 128 * tile + 128] = rows
    for base, q_ref, o_ref in ((DEP, dq_ref, do_ref), (TIM, tq_ref, to_ref)):
        for tile in range(12):
            rows = att_ref[base + 192 * tile : base + 192 * tile + 192, :].astype(F32)
            if tile < 9:
                q_ref[:, 128 * tile : 128 * tile + 128] = rows
            else:
                o_ref[:, 128 * (tile - 9) : 128 * (tile - 9) + 128] = rows
    if own:
        first_ref, second_ref, dscale_ref, tscale_ref = refs[7:11]
        two = ffn_ref[FFN : FFN + 32, :].astype(F32)
        dep = att_ref[DEP + ATT : DEP + ATT + 32, :].astype(F32)
        tim = att_ref[TIM + ATT : TIM + ATT + 32, :].astype(F32)
        one = dep + tim
        for tile in range(3):
            lanes = slice(128 * tile, 128 * tile + 128)
            second_ref[lanes] = two[8 * tile : 8 * tile + 1].reshape(128)
            first_ref[lanes] = one[8 * tile : 8 * tile + 1].reshape(128)
        for head in range(6):
            dscale_ref[head] = dep[24 + head // 2, 64 * (head % 2)]
            tscale_ref[head] = tim[24 + head // 2, 64 * (head % 2)]


def unpack(own, me, gathered, partial=()):
    half = (lambda m: m[0]) if own else (lambda m: 1 - m[0])
    out_shape = [
        shape((C, 3 * C), F32),
        shape((C, C), F32),
        shape((C, 3 * C), F32),
        shape((C, C), F32),
        shape((C, HID), F32),
        shape((3, 3, 3, HID), F32),
        shape((HID, C), F32),
    ]
    out_specs = [
        pl.BlockSpec((192, 3 * C), lambda i, m: (half(m), 0)),
        pl.BlockSpec((192, C), lambda i, m: (half(m), 0)),
        pl.BlockSpec((192, 3 * C), lambda i, m: (half(m), 0)),
        pl.BlockSpec((192, C), lambda i, m: (half(m), 0)),
        pl.BlockSpec((C, HID // 2), lambda i, m: (0, half(m))),
        pl.BlockSpec((3, 3, 3, HID // 2), lambda i, m: (0, 0, 0, half(m))),
        pl.BlockSpec((HID // 2, C), lambda i, m: (half(m), 0)),
    ]
    if own:
        out_shape += [shape((C,), F32), shape((C,), F32), shape((6,), F32), shape((6,), F32)]
        out_specs += [pl.BlockSpec((C,), lambda i, m: (0,))] * 2 + [pl.BlockSpec(memory_space=pltpu.SMEM)] * 2
    return pl.pallas_call(
        functools.partial(unpack_kernel, own),
        out_shape=tuple(out_shape),
        grid_spec=pltpu.PrefetchScalarGridSpec(
            num_scalar_prefetch=1,
            grid=(1,),
            in_specs=[pl.BlockSpec((COPIES, 2 * CHUNK, 128), lambda i, m: (0, 0, 0))]
            + [pl.BlockSpec(memory_space=pl.ANY)] * len(partial),
            out_specs=tuple(out_specs),
            scratch_shapes=[pltpu.VMEM((STACK, 128), BF16), pltpu.VMEM((STACK, 128), BF16)],
        ),
        input_output_aliases={2 + i: i for i in range(len(partial))},
        name="unpack_own" if own else "unpack_other",
    )(me, gathered, *partial)


def local(
    tokens, out_grad, first_gain, depth_qkv, depth_out, time_qkv, time_out, second_gain, up_weight,
    spatial_kernel, down_weight, depth_scale, time_scale,
):
    pd = jnp.asarray(spread_depth(), BF16)
    pt = jnp.asarray(spread_time(), BF16)
    gd = jnp.asarray(groups_depth())
    gt = jnp.asarray(groups_time())
    me = jnp.stack([lax.axis_index("core"), lax.axis_index(TA), lax.axis_index(DEV)]).astype(jnp.int32)
    block_shape = tokens.shape
    flat = tokens.reshape(ROWS, C)
    og = out_grad.reshape(ROWS, C)
    count, frames = lax.axis_size(DEV), lax.axis_size(TA)
    ahead = [(i, i + 1) for i in range(count - 1)]
    behind = [(i + 1, i) for i in range(count - 1)]

    queue = []

    def exchange(values, axes):
        if queue:
            values, _ = lax.optimization_barrier((values, queue[-1]))
        queue.append(lax.all_to_all(values, axes, split_axis=0, concat_axis=0, tiled=True))
        return queue[-1]

    dep, tim = first_norm(flat, first_gain, pd, pt)
    tim = [exchange(tim, TA)]
    dep = [exchange(dep, DEV)]
    tim_out, tim_fields, tim_mixed = attend(tim, time_qkv, time_out, time_scale, gt)
    tim_back = exchange(tim_out[0], TA)
    dep_out, dep_fields, dep_mixed = attend(dep, depth_qkv, depth_out, depth_scale, gd)
    dep_back = exchange(dep_out[0], DEV)
    og_low = lax.ppermute(og[CELLS:], DEV, ahead)
    og_high = lax.ppermute(og[:CELLS], DEV, behind)
    dep_back, og_low, og_high = lax.optimization_barrier((dep_back, og_low, og_high))
    mid = middle_of(flat, dep_back, tim_back, pd, pt)
    low = lax.ppermute(mid, DEV, ahead)
    high = lax.ppermute(mid, DEV, behind)
    block_out, mgrad, ffn_g, bdep, btim = feed_forward(
        low, mid, high, og_low, og, og_high, second_gain, up_weight, spatial_kernel, down_weight, pd, pt
    )
    btim = exchange(btim, TA)
    bdep = exchange(bdep, DEV)
    ffn_other = swapped(ffn_g)
    ffn_stack = pair_sum(me, [ffn_g, ffn_other])
    ffn_stack = exchange(ffn_stack.reshape(COPIES, CHUNK, 128), CHIPS)
    (tim_first,), tim_g = attend_back(
        me, [btim], tim, tim_fields, tim_mixed, time_qkv, time_out, time_scale, gt, first_gain, 1
    )
    tim_other = swapped(tim_g)
    dep_first, dep_g = attend_back(
        me, [bdep], dep, dep_fields, dep_mixed, depth_qkv, depth_out, depth_scale, gd, first_gain, 16
    )
    dep_other = swapped(dep_g)
    tim_first = exchange(tim_first, TA)
    factor = 1.0 / math.sqrt(ROWS * count * frames)
    att_stack = pair_sum(me, [dep_g, dep_other, tim_g, tim_other])
    att_stack = exchange(att_stack.reshape(COPIES, CHUNK, 128), CHIPS)
    ffn_chunk = chip_sum(ffn_stack, factor)
    dep_first = [
        lax.ppermute(part, DEV, [(i, (i + step) % count) for i in range(count)]) if step else part
        for step, part in enumerate(dep_first)
    ]
    spread = chip_spread(att_stack, ffn_chunk, factor)
    own = exchange(spread, CHIPS)
    input_grad = last_norm(me, flat, dep_first, tim_first, pd, pt, first_gain, mgrad)
    other = swapped(own)
    *partial, first_gain_grad, second_gain_grad, depth_scale_grad, time_scale_grad = unpack(True, me, own)
    dq, do, tq, to, up_g, kern_g, down_g = unpack(False, me, other, partial)
    return (
        block_out.reshape(block_shape),
        input_grad.reshape(block_shape),
        dq,
        do,
        tq,
        to,
        up_g,
        kern_g,
        down_g,
        first_gain_grad,
        second_gain_grad,
        depth_scale_grad,
        time_scale_grad,
    )


def solution(mesh):
    fine = Mesh(mesh.devices.reshape(4, 2, 2, 2, 4), ("y", "xh", "core", "xl", "z"))
    split = P(TA, DEV, None, None)
    return jax.shard_map(
        local,
        mesh=fine,
        in_specs=(split, split) + (P(),) * 11,
        out_specs=(split, split) + (P(),) * 11,
        check_vma=False,
    )
```

```python
import functools
import math

import jax
import jax.numpy as jnp
from jax import lax
from jax.experimental import pallas as pl
from jax.experimental.pallas import tpu as pltpu
from jax.sharding import Mesh
from jax.sharding import PartitionSpec as P


C = 384
HID = 1536
PW = 24
CELLS = 144
ROWS = 288
BLOCK = 256
STEPS = HID // BLOCK
PAD = 192
DEV = ("y", "xh", "core")
TA = ("xl", "z")
CHIPS = ("y", "xh", "xl", "z")
COPIES = 64
CHUNK = 152
F32 = jnp.float32
BF16 = jnp.bfloat16
EPS = 1e-5


def piece_of(row, size):
    return (row * (65536 // size + 1)) >> 16


def spread(size, cells):
    row = lax.broadcasted_iota(jnp.int32, (size * (CELLS // cells), 1), 0)
    owner = piece_of(row, size)
    k = row - size * owner
    token = k + cells * owner + jnp.where(k >= cells, CELLS - cells, 0)
    token = jnp.where(k < 2 * cells, token, -1)
    lane = lax.broadcasted_iota(jnp.int32, (row.shape[0], ROWS), 1)
    return jnp.where(token == lane, 1.0, 0.0).astype(BF16)


def spread_depth():
    return spread(24, 9)


def spread_time():
    return spread(40, 18)


def same_group(rows):
    def group(index):
        if rows == 320:
            return index - 40 * piece_of(index, 40)
        k = index - 24 * piece_of(index, 24)
        return jnp.where(k >= 9, k - 9, k) + jnp.where(k >= 18, 9, 0)

    left = group(lax.broadcasted_iota(jnp.int32, (rows, 1), 0))
    right = group(lax.broadcasted_iota(jnp.int32, (1, rows), 1))
    return jnp.where(left == right, 1.0, 0.0)


def dot(left, right, dims=((1,), (0,)), precision=None):
    return lax.dot_general(
        left, right, (dims, ((), ())), preferred_element_type=F32, precision=precision
    )


def norm_parts(values):
    centered = values - jnp.mean(values, axis=-1, keepdims=True)
    inverse = lax.rsqrt(jnp.mean(centered * centered, axis=-1, keepdims=True) + EPS)
    return centered * inverse, inverse


def norm_back(scaled, inverse, grads):
    mean = jnp.mean(grads, axis=-1, keepdims=True)
    along = jnp.mean(grads * scaled, axis=-1, keepdims=True)
    return (grads - mean - scaled * along) * inverse


def vmem(count):
    return [pl.BlockSpec(memory_space=pltpu.VMEM)] * count


SMEM = [pl.BlockSpec(memory_space=pltpu.SMEM)]


def shape(dims, kind=BF16):
    return jax.ShapeDtypeStruct(dims, kind)


def deal(values, turn, mask, part_refs, hold_ref):
    count = len(part_refs)
    hold_ref[...] = values.reshape(count, values.shape[0] // count, C)
    for step, ref in enumerate(part_refs):
        ref[...] = hold_ref[(turn + step) & mask].astype(BF16)


def row_of(ref):
    return ref[...].reshape(1, ref.shape[0])


def first_kernel(tok_ref, gain_ref, dep_ref, tim_ref):
    scaled, _ = norm_parts(tok_ref[...].astype(F32))
    normed = (scaled * row_of(gain_ref)).astype(BF16)
    dep_ref[...] = dot(spread_depth(), normed).reshape(16, 24, C).astype(BF16)
    tim_ref[...] = dot(spread_time(), normed).reshape(8, 40, C).astype(BF16)


def first_norm(tokens, gain):
    return pl.pallas_call(
        first_kernel,
        out_shape=(shape((16, 24, C)), shape((8, 40, C))),
        in_specs=vmem(2),
        out_specs=tuple(vmem(2)),
        name="first_norm",
    )(tokens, gain)


ATT = 2304


def lane_is_low():
    return lax.broadcasted_iota(jnp.int32, (1, 128), 1) < 64


def head_ones():
    row = lax.broadcasted_iota(jnp.int32, (128, 128), 0) < 64
    col = lax.broadcasted_iota(jnp.int32, (128, 128), 1) < 64
    return jnp.where(row == col, 1.0, 0.0).astype(BF16)


def head_sum(values, ones):
    high = values.astype(BF16)
    low = (values - high.astype(F32)).astype(BF16)
    return dot(high, ones) + dot(low, ones)


def joined(ref):
    count, part, _ = ref.shape
    return ref[...].astype(F32).reshape(count * part, C).astype(BF16)


def attend_kernel(in_ref, w_ref, wo_ref, scale_ref, out_ref, fields_ref, mixed_ref, same_ref):
    rowed = joined(in_ref)
    rows = rowed.shape[0]
    fields_ref[...] = dot(rowed, w_ref[...]).astype(BF16)
    same_ref[...] = same_group(rows)
    ones = head_ones()
    low = lane_is_low()
    side = jnp.ones((rows, 128), BF16)

    def one_pair(pair, _):
        at = pl.multiple_of(128 * pair, 128)
        query = fields_ref[:, pl.ds(at, 128)].astype(F32)
        keyed = fields_ref[:, pl.ds(C + at, 128)].astype(F32)
        valued = fields_ref[:, pl.ds(2 * C + at, 128)]
        query = query * lax.rsqrt(head_sum(query * query, ones) + 1e-6)
        keyed = (keyed * lax.rsqrt(head_sum(keyed * keyed, ones) + 1e-6)).astype(BF16)
        query = query * jnp.where(low, scale_ref[2 * pair], scale_ref[2 * pair + 1])
        both = jnp.concatenate([valued, side], axis=1)
        results = []
        for half in range(2):
            mine = low if half == 0 else jnp.logical_not(low)
            scores = dot(jnp.where(mine, query, 0.0).astype(BF16), keyed, ((1,), (1,)))
            weights = (jnp.exp(scores) * same_ref[...]).astype(BF16)
            sums = dot(weights, both)
            results.append(sums[:, :128] / sums[:, 128:])
        mixed_ref[:, pl.ds(at, 128)] = jnp.where(low, results[0], results[1]).astype(BF16)
        return 0

    lax.fori_loop(0, 3, one_pair, 0)
    out_ref[...] = dot(mixed_ref[...], wo_ref[...]).reshape(out_ref.shape).astype(BF16)


def attend(inputs, weight, out_weight, scale):
    rows = inputs.shape[0] * inputs.shape[1]
    return pl.pallas_call(
        attend_kernel,
        out_shape=(shape(inputs.shape), shape((rows, 3 * C)), shape((rows, C))),
        in_specs=vmem(3) + SMEM,
        out_specs=tuple(vmem(3)),
        scratch_shapes=[pltpu.VMEM((rows, rows), F32)],
    )(inputs, weight, out_weight, scale)


def put_tile(ref, tile, values):
    for half in range(2):
        ref[half, 192 * tile : 192 * tile + 192, :] = values[192 * half : 192 * half + 192].astype(BF16)


def wide(values, lanes):
    return jnp.concatenate([values] * 3, axis=1)[:, :lanes]


def attend_back_kernel(grad_ref, in_ref, me_ref, fields_ref, mixed_ref, w_ref, wo_ref, scale_ref, gain_ref, *refs):
    count = in_ref.shape[0]
    out_refs, (weights_ref, small_ref, same_ref, fg_ref, cot_ref, hold_ref) = refs[:count], refs[count:]
    grads = joined(grad_ref)
    rows = grads.shape[0]
    same_ref[...] = same_group(rows)
    out_grad = dot(mixed_ref[...], grads, ((0,), (0,)))
    for tile in range(3):
        put_tile(weights_ref, 9 + tile, out_grad[:, 128 * tile : 128 * tile + 128])
    cot_ref[...] = dot(grads, wo_ref[...], ((1,), (1,))).astype(BF16)
    ones = head_ones()
    low = lane_is_low()
    side = jnp.ones((rows, 128), BF16)
    full = jnp.ones((128, 128), BF16)
    small_ref[24:32, :] = jnp.zeros((8, 128), F32)

    def one_pair(pair, _):
        at = pl.multiple_of(128 * pair, 128)
        query = fields_ref[:, pl.ds(at, 128)].astype(F32)
        keyed = fields_ref[:, pl.ds(C + at, 128)].astype(F32)
        valued = fields_ref[:, pl.ds(2 * C + at, 128)]
        query_inv = lax.rsqrt(head_sum(query * query, ones) + 1e-6)
        keyed_inv = lax.rsqrt(head_sum(keyed * keyed, ones) + 1e-6)
        query = query * query_inv
        keyed = keyed * keyed_inv
        scale = jnp.where(low, scale_ref[2 * pair], scale_ref[2 * pair + 1])
        scaled = query * scale
        keyed_short = keyed.astype(BF16)
        cot = cot_ref[:, pl.ds(at, 128)]
        along = cot.astype(F32) * mixed_ref[:, pl.ds(at, 128)].astype(F32)
        query_grad = jnp.zeros((rows, 128), F32)
        keyed_grad = jnp.zeros((rows, 128), F32)
        value_grad = jnp.zeros((rows, 128), F32)
        for half in range(2):
            mine = low if half == 0 else jnp.logical_not(low)
            delta = wide(head_sum(jnp.where(mine, along, 0.0), full), rows)
            mine_query = jnp.where(mine, scaled, 0.0).astype(BF16)
            mine_cot = jnp.where(mine, cot.astype(F32), 0.0).astype(BF16)
            mine_keyed = jnp.where(mine, keyed, 0.0).astype(BF16)
            scores = dot(mine_query, keyed_short, ((1,), (1,)))
            weights = jnp.exp(scores) * same_ref[...]
            total = dot(weights.astype(BF16), side)
            weights = weights * wide(1.0 / total, rows)
            weights_grad = dot(mine_cot, valued, ((1,), (1,)))
            scores_grad = (weights * (weights_grad - delta)).astype(BF16)
            value_grad = value_grad + dot(weights.astype(BF16), mine_cot, ((0,), (0,)))
            query_grad = query_grad + dot(scores_grad, mine_keyed)
            keyed_grad = keyed_grad + dot(scores_grad, mine_query, ((0,), (0,)))
        total = jnp.sum(query_grad * query, axis=0, keepdims=True)
        small_ref[pl.ds(24 + pair, 1), :] = head_sum(jnp.broadcast_to(total, (8, 128)), ones)[:1]
        query_grad = query_grad * scale
        query_grad = (query_grad - query * head_sum(query * query_grad, ones)) * query_inv
        keyed_grad = (keyed_grad - keyed * head_sum(keyed * keyed_grad, ones)) * keyed_inv
        fg_ref[:, pl.ds(at, 128)] = query_grad.astype(BF16)
        fg_ref[:, pl.ds(C + at, 128)] = keyed_grad.astype(BF16)
        fg_ref[:, pl.ds(2 * C + at, 128)] = value_grad.astype(BF16)
        return 0

    lax.fori_loop(0, 3, one_pair, 0)
    back = dot(fg_ref[...], w_ref[...], ((1,), (1,)))
    deal(back, me_ref[count // 8 - 1], count - 1, out_refs, hold_ref)
    rowed = joined(in_ref)
    grad = dot(rowed, fg_ref[...], ((0,), (0,)))
    for tile in range(9):
        put_tile(weights_ref, tile, grad[:, 128 * tile : 128 * tile + 128])
    gain_part = jnp.sum(back * rowed.astype(F32), axis=0, keepdims=True) / row_of(gain_ref)
    small_ref[0:24, :] = jnp.zeros((24, 128), F32)
    for tile in range(3):
        small_ref[8 * tile : 8 * tile + 1, :] = gain_part[:, 128 * tile : 128 * tile + 128]
    for half in range(2):
        weights_ref[half, ATT:, :] = small_ref[...].astype(BF16)


def attend_back(me, grads, inputs, fields, mixed, weight, out_weight, scale, gain):
    count, part, _ = inputs.shape
    rows = count * part
    outs = pl.pallas_call(
        attend_back_kernel,
        out_shape=(shape((part, C)),) * count + (shape((2, ATT + 32, 128)),),
        in_specs=vmem(2) + SMEM + vmem(4) + SMEM + vmem(1),
        out_specs=tuple(vmem(count + 1)),
        scratch_shapes=[
            pltpu.VMEM((32, 128), F32),
            pltpu.VMEM((rows, rows), F32),
            pltpu.VMEM((rows, 3 * C), BF16),
            pltpu.VMEM((rows, C), BF16),
            pltpu.VMEM((count, part, C), F32),
        ],
    )(grads, inputs, me, fields, mixed, weight, out_weight, scale, gain)
    return outs[:count], outs[count]


def middle_kernel(tok_ref, dep_ref, tim_ref, out_ref):
    total = tok_ref[...].astype(F32) + dot(spread_depth(), joined(dep_ref), ((0,), (0,)))
    out_ref[...] = (total + dot(spread_time(), joined(tim_ref), ((0,), (0,)))).astype(BF16)


def middle_of(tokens, depth, time):
    return pl.pallas_call(
        middle_kernel,
        out_shape=shape((ROWS, C)),
        in_specs=vmem(3),
        out_specs=vmem(1)[0],
        name="middle",
    )(tokens, depth, time)


STRIDE = 1600
FFN = 3 * STRIDE


def down_one(values, first):
    return jnp.where(first, 0.0, pltpu.roll(values, 1, 0))


def up_one(values, last):
    return jnp.where(last, 0.0, pltpu.roll(values, PW - 1, 0))


def act_pair(values):
    square = values * values
    inner = 0.7978845608 * values * (1.0 + 0.044715 * square)
    tanh = jnp.tanh(inner)
    half = 0.5 * (1.0 + tanh)
    slope = 0.7978845608 * (1.0 + 3.0 * 0.044715 * square)
    return values * half, half + 0.5 * values * (1.0 - tanh * tanh) * slope


def feed_kernel(
    low_ref, mid_ref, high_ref, og_low_ref, og_ref, og_high_ref, gain_ref, up_ref, kern_ref, down_ref,
    block_ref, mgrad_ref, bdep_ref, btim_ref, own_ref, hid_out, fgr_out, act_out, hgr_out,
    norm_ref, og4_ref, hid_ref, fgr_ref, act_ref, hgr_ref, ag_ref, block_acc, back_acc,
):
    step = pl.program_id(0)

    @pl.when(step == 0)
    def _():
        for at, ref in ((0, low_ref), (ROWS, mid_ref), (2 * ROWS, high_ref)):
            scaled, _ = norm_parts(ref[...].astype(F32))
            norm_ref[at : at + ROWS, :] = (scaled * row_of(gain_ref)).astype(BF16)
        og4_ref[0:CELLS, :] = og_low_ref[...]
        og4_ref[CELLS : CELLS + ROWS, :] = og_ref[...]
        og4_ref[CELLS + ROWS : 2 * ROWS, :] = og_high_ref[...]
        hid_ref[...] = jnp.zeros(hid_ref.shape, F32)
        fgr_ref[...] = jnp.zeros(fgr_ref.shape, F32)
        block_acc[...] = jnp.zeros(block_acc.shape, F32)
        back_acc[...] = jnp.zeros(back_acc.shape, F32)
        own_ref[...] = norm_ref[ROWS : 2 * ROWS, :]

    place = lax.broadcasted_iota(jnp.int32, (PW, 128), 0)
    first, last = place == 0, place == PW - 1
    short = dot(norm_ref[...], up_ref[...]).astype(BF16)
    hid_out[...] = short[CELLS : 5 * CELLS]
    hidden = short.astype(F32)
    ag_ref[...] = dot(og4_ref[...], down_ref[...], ((1,), (1,)))
    for lt in range(2):
        for piece in range(6):
            hid_ref[lt, piece * PAD + PW : piece * PAD + PW + CELLS, :] = hidden[
                piece * CELLS : (piece + 1) * CELLS, 128 * lt : 128 * lt + 128
            ]

    for lt in range(2):
        lanes = slice(128 * lt, 128 * lt + 128)

        def forward(piece, _, lt=lt, lanes=lanes):
            for i in range(6):
                acc = [None] * 3
                for a in range(3):
                    for b in range(3):
                        start = pl.multiple_of((piece + a) * PAD + PW * (i + b), 8)
                        window = hid_ref[lt, pl.ds(start, PW), :]
                        for e in range(3):
                            term = kern_ref[a, b, e : e + 1, lanes] * window
                            acc[e] = term if acc[e] is None else acc[e] + term
                filtered = acc[1] + down_one(acc[0], first) + up_one(acc[2], last)
                value, slope = act_pair(filtered)
                at = pl.multiple_of(piece * CELLS + PW * i, 8)
                grad = (ag_ref[pl.ds(at, PW), lanes] * slope).astype(BF16).astype(F32)
                fgr_ref[lt, pl.ds(pl.multiple_of(piece * PAD + PW * (i + 1), 8), PW), :] = grad
                act_ref[pl.ds(at, PW), lanes] = value
            return 0

        lax.fori_loop(0, 4, forward, 0)

        def backward(piece, sums, lt=lt, lanes=lanes):
            sums = list(sums)
            for i in range(6):
                acc = [None] * 3
                for a in range(3):
                    for b in range(3):
                        start = pl.multiple_of((piece + 2 - a) * PAD + PW * (i + 2 - b), 8)
                        window = fgr_ref[lt, pl.ds(start, PW), :]
                        for e in range(3):
                            term = kern_ref[a, b, e : e + 1, lanes] * window
                            acc[e] = term if acc[e] is None else acc[e] + term
                total = acc[1] + up_one(acc[0], last) + down_one(acc[2], first)
                hgr_ref[pl.ds(pl.multiple_of(piece * CELLS + PW * i, 8), PW), lanes] = total
            return tuple(sums)

        lax.fori_loop(0, 2, backward, ())

    for lt in range(2):
        for piece in range(2):
            at = (piece + 1) * PAD + PW
            fgr_out[piece * CELLS : piece * CELLS + CELLS, 128 * lt : 128 * lt + 128] = fgr_ref[
                lt, at : at + CELLS, :
            ].astype(BF16)
    active = act_ref[CELLS : CELLS + ROWS, :].astype(BF16)
    act_out[...] = active
    block_acc[...] += dot(active, down_ref[...])
    hidden_grad = hgr_ref[...].astype(BF16)
    hgr_out[...] = hidden_grad
    back_acc[...] += dot(hidden_grad, up_ref[...], ((1,), (1,)))

    @pl.when(step == STEPS - 1)
    def _():
        wide = mid_ref[...].astype(F32)
        block_ref[...] = (wide + block_acc[...]).astype(BF16)
        scaled, inverse = norm_parts(wide)
        back = norm_back(scaled, inverse, back_acc[...] * row_of(gain_ref))
        middle_grad = og_ref[...].astype(F32) + back
        mgrad_ref[...] = middle_grad
        short = middle_grad.astype(BF16)
        bdep_ref[...] = dot(spread_depth(), short).reshape(16, 24, C).astype(BF16)
        btim_ref[...] = dot(spread_time(), short).reshape(8, 40, C).astype(BF16)


def grads_kernel(
    og_ref, own_ref, hid_in, fgr_in, act_in, hgr_in, up_ref, gain_ref, weights_ref, hid_ref, fgr_ref, prod_acc, kgrad_ref
):
    step = pl.program_id(0)

    @pl.when(step == 0)
    def _():
        hid_ref[...] = jnp.zeros(hid_ref.shape, F32)
        prod_acc[...] = jnp.zeros(prod_acc.shape, F32)

    place = lax.broadcasted_iota(jnp.int32, (PW, 128), 0)
    first, last = place == 0, place == PW - 1
    for lt in range(2):
        lanes = slice(128 * lt, 128 * lt + 128)
        fgr_ref[lt] = fgr_in[:, lanes].astype(F32)
        for piece in range(4):
            hid_ref[lt, piece * PAD + PW : piece * PAD + PW + CELLS, :] = hid_in[
                piece * CELLS : piece * CELLS + CELLS, lanes
            ].astype(F32)

    for lt in range(2):
        for a in range(3):

            def products(piece, sums, a=a, lt=lt):
                sums = list(sums)
                for i in range(6):
                    own = pl.multiple_of(piece * CELLS + PW * i, 8)
                    grad = fgr_ref[lt, pl.ds(own, PW), :]
                    shifted = (up_one(grad, last), grad, down_one(grad, first))
                    for b in range(3):
                        start = pl.multiple_of((piece + a) * PAD + PW * (i + b), 8)
                        window = hid_ref[lt, pl.ds(start, PW), :]
                        for e in range(3):
                            term = window * shifted[e]
                            k = 3 * b + e
                            sums[k] = sums[k] + (term[0:8] + term[8:16] + term[16:24])
                return tuple(sums)

            sums = lax.fori_loop(0, 2, products, tuple(jnp.zeros((8, 128), F32) for _ in range(9)))
            for k in range(9):
                row = 32 * lt + 9 * a + k
                kgrad_ref[row : row + 1, :] = jnp.sum(sums[k], axis=0, keepdims=True)
        kgrad_ref[32 * lt + 27 : 32 * lt + 32, :] = jnp.zeros((5, 128), F32)

    down_grad = dot(act_in[...], og_ref[...], ((0,), (0,)))
    up_grad = dot(own_ref[...], hgr_in[...], ((0,), (0,)))
    product = up_grad * up_ref[...].astype(F32)
    prod_acc[...] += product[:, :128] + product[:, 128:]
    half = step // 3
    base = pl.multiple_of((step - 3 * half) * STRIDE, 16)
    for tile in range(2):
        weights_ref[half, pl.ds(base + C * tile, C), :] = up_grad[:, 128 * tile : 128 * tile + 128].astype(BF16)
    for tile in range(3):
        at = 2 * C + BLOCK * tile
        weights_ref[half, pl.ds(base + at, BLOCK), :] = down_grad[:, 128 * tile : 128 * tile + 128].astype(BF16)
    weights_ref[half, pl.ds(base + 1536, 64), :] = kgrad_ref[...].astype(BF16)

    @pl.when(step == STEPS - 1)
    def _():
        part = dot(jnp.ones((8, 128), F32), prod_acc[...], ((1,), (1,)), lax.Precision.HIGHEST)
        part = part / row_of(gain_ref)
        for tile in range(3):
            kgrad_ref[8 * tile : 8 * tile + 8, :] = part[:, 128 * tile : 128 * tile + 128]
        kgrad_ref[24:32, :] = jnp.zeros((8, 128), F32)
        for side in range(2):
            weights_ref[side, 3 * STRIDE :, :] = kgrad_ref[0:32, :].astype(BF16)


def feed_grads(og, own, hid, fgr, act, hgr, up, gain):
    def column(rows):
        return pl.BlockSpec((rows, BLOCK), lambda s: (0, s))

    return pl.pallas_call(
        grads_kernel,
        grid=(STEPS,),
        out_shape=shape((2, FFN + 32, 128)),
        in_specs=[
            pl.BlockSpec((ROWS, C), lambda s: (0, 0)),
            pl.BlockSpec((ROWS, C), lambda s: (0, 0)),
            column(2 * ROWS),
            column(ROWS),
            column(ROWS),
            column(ROWS),
            column(C),
            pl.BlockSpec((C,), lambda s: (0,)),
        ],
        out_specs=pl.BlockSpec((2, FFN + 32, 128), lambda s: (0, 0, 0)),
        scratch_shapes=[
            pltpu.VMEM((2, 4 * PAD, 128), F32),
            pltpu.VMEM((2, ROWS, 128), F32),
            pltpu.VMEM((C, 128), F32),
            pltpu.VMEM((64, 128), F32),
        ],
        name="feed_grads",
    )(og, own, hid, fgr, act, hgr, up, gain)


def feed_forward(low, mid, high, og_low, og, og_high, gain, up, kern, down):
    def whole(*dims):
        return pl.BlockSpec(dims, lambda s: (0,) * len(dims))

    return pl.pallas_call(
        feed_kernel,
        grid=(STEPS,),
        out_shape=(
            shape((ROWS, C)),
            shape((ROWS, C), F32),
            shape((16, 24, C)),
            shape((8, 40, C)),
            shape((ROWS, C)),
            shape((2 * ROWS, HID)),
            shape((ROWS, HID)),
            shape((ROWS, HID)),
            shape((ROWS, HID)),
        ),
        in_specs=[
            whole(ROWS, C),
            whole(ROWS, C),
            whole(ROWS, C),
            whole(CELLS, C),
            whole(ROWS, C),
            whole(CELLS, C),
            whole(C),
            pl.BlockSpec((C, BLOCK), lambda s: (0, s)),
            pl.BlockSpec((3, 3, 3, BLOCK), lambda s: (0, 0, 0, s)),
            pl.BlockSpec((BLOCK, C), lambda s: (s, 0)),
        ],
        out_specs=(
            whole(ROWS, C),
            whole(ROWS, C),
            whole(16, 24, C),
            whole(8, 40, C),
            whole(ROWS, C),
            pl.BlockSpec((2 * ROWS, BLOCK), lambda s: (0, s)),
            pl.BlockSpec((ROWS, BLOCK), lambda s: (0, s)),
            pl.BlockSpec((ROWS, BLOCK), lambda s: (0, s)),
            pl.BlockSpec((ROWS, BLOCK), lambda s: (0, s)),
        ),
        scratch_shapes=[
            pltpu.VMEM((3 * ROWS, C), BF16),
            pltpu.VMEM((2 * ROWS, C), BF16),
            pltpu.VMEM((2, 6 * PAD, 128), F32),
            pltpu.VMEM((2, 4 * PAD, 128), F32),
            pltpu.VMEM((2 * ROWS, BLOCK), F32),
            pltpu.VMEM((ROWS, BLOCK), F32),
            pltpu.VMEM((2 * ROWS, BLOCK), F32),
            pltpu.VMEM((ROWS, C), F32),
            pltpu.VMEM((ROWS, C), F32),
        ],
        name="feed_forward",
    )(low, mid, high, og_low, og, og_high, gain, up, kern, down)


def last_kernel(me_ref, tok_ref, gain_ref, mgrad_ref, *rest):
    dep_refs, tim_refs, (out_ref, dep_hold, tim_hold) = rest[:16], rest[16:24], rest[24:]
    for step, ref in enumerate(dep_refs):
        dep_hold[(me_ref[1] - step) & 15] = ref[...].astype(F32)
    for step, ref in enumerate(tim_refs):
        tim_hold[(me_ref[0] - step) & 7] = ref[...].astype(F32)
    dep = dep_hold[...].reshape(384, C).astype(BF16)
    tim = tim_hold[...].reshape(320, C).astype(BF16)
    back = dot(spread_depth(), dep, ((0,), (0,))) + dot(spread_time(), tim, ((0,), (0,)))
    scaled, inverse = norm_parts(tok_ref[...].astype(F32))
    out_ref[...] = (mgrad_ref[...] + norm_back(scaled, inverse, back * row_of(gain_ref))).astype(BF16)


def last_norm(me, tokens, depth, time, gain, mgrad):
    return pl.pallas_call(
        last_kernel,
        out_shape=shape((ROWS, C)),
        in_specs=SMEM + vmem(27),
        out_specs=vmem(1)[0],
        scratch_shapes=[pltpu.VMEM((16, 24, C), F32), pltpu.VMEM((8, 40, C), F32)],
        name="last_norm",
    )(me, tokens, gain, mgrad, *depth, *time)


STACK = COPIES * CHUNK
DEP = FFN + 32
TIM = DEP + ATT + 32


def pair_kernel(me_ref, *refs):
    out_ref, at = refs[-1], 0
    for one, two in zip(refs[0:-1:2], refs[1:-1:2], strict=True):
        size = one.shape[1]
        out_ref[at : at + size, :] = (one[0].astype(F32) + two[0].astype(F32)).astype(BF16)
        at += size
    out_ref[at:, :] = jnp.zeros((STACK - at, 128), BF16)


def swapped(array):
    return lax.ppermute(array, "core", [(0, 1), (1, 0)])


def pair_sum(me, args):
    return pl.pallas_call(
        pair_kernel,
        out_shape=shape((STACK, 128)),
        grid_spec=pltpu.PrefetchScalarGridSpec(
            num_scalar_prefetch=1,
            grid=(1,),
            in_specs=[pl.BlockSpec((1,) + a.shape[1:], lambda i, m: (m[2], 0, 0)) for a in args],
            out_specs=pl.BlockSpec((STACK, 128), lambda i, m: (0, 0)),
        ),
    )(me, *args)


def chip_kernel(factor, in_ref, out_ref):
    def add(source, total):
        return total + in_ref[source].astype(F32)

    total = lax.fori_loop(1, COPIES, add, in_ref[0].astype(F32), unroll=3)
    total = (total * factor).astype(BF16)

    def put(target, _):
        out_ref[target] = total
        return 0

    lax.fori_loop(0, COPIES, put, 0, unroll=2)


def chip_sum(received, factor):
    return pl.pallas_call(
        functools.partial(chip_kernel, factor),
        out_shape=shape(received.shape),
        in_specs=vmem(1),
        out_specs=vmem(1)[0],
        name="chip_sum",
    )(received)


def unpack_kernel(own, me_ref, in_ref, *refs):
    refs = refs if own else refs[7:]
    dq_ref, do_ref, tq_ref, to_ref, up_ref, kg_ref, dn_ref = refs[:7]
    for step in range(3):
        at = STRIDE * step
        for tile in range(2):
            lanes = slice(BLOCK * step + 128 * tile, BLOCK * step + 128 * tile + 128)
            up_ref[:, lanes] = in_ref[at + C * tile : at + C * tile + C, :].astype(F32)
            kgrad = in_ref[at + 1536 + 32 * tile : at + 1568 + 32 * tile, :].astype(F32)
            for k in range(27):
                kg_ref[k // 9, k // 3 % 3, k % 3 : k % 3 + 1, lanes] = kgrad[k : k + 1]
        for tile in range(3):
            rows = in_ref[at + 768 + BLOCK * tile : at + 1024 + BLOCK * tile, :].astype(F32)
            dn_ref[BLOCK * step : BLOCK * step + BLOCK, 128 * tile : 128 * tile + 128] = rows
    for base, q_ref, o_ref in ((DEP, dq_ref, do_ref), (TIM, tq_ref, to_ref)):
        for tile in range(12):
            rows = in_ref[base + 192 * tile : base + 192 * tile + 192, :].astype(F32)
            if tile < 9:
                q_ref[:, 128 * tile : 128 * tile + 128] = rows
            else:
                o_ref[:, 128 * (tile - 9) : 128 * (tile - 9) + 128] = rows
    if own:
        first_ref, second_ref, dscale_ref, tscale_ref = refs[7:11]
        two = in_ref[FFN : FFN + 32, :].astype(F32)
        dep = in_ref[DEP + ATT : DEP + ATT + 32, :].astype(F32)
        tim = in_ref[TIM + ATT : TIM + ATT + 32, :].astype(F32)
        one = dep + tim
        for tile in range(3):
            lanes = slice(128 * tile, 128 * tile + 128)
            second_ref[lanes] = two[8 * tile : 8 * tile + 1].reshape(128)
            first_ref[lanes] = one[8 * tile : 8 * tile + 1].reshape(128)
        for head in range(6):
            dscale_ref[head] = dep[24 + head // 2, 64 * (head % 2)]
            tscale_ref[head] = tim[24 + head // 2, 64 * (head % 2)]


def unpack(own, me, gathered, partial=()):
    half = (lambda m: m[2]) if own else (lambda m: 1 - m[2])
    out_shape = [
        shape((C, 3 * C), F32),
        shape((C, C), F32),
        shape((C, 3 * C), F32),
        shape((C, C), F32),
        shape((C, HID), F32),
        shape((3, 3, 3, HID), F32),
        shape((HID, C), F32),
    ]
    out_specs = [
        pl.BlockSpec((192, 3 * C), lambda i, m: (half(m), 0)),
        pl.BlockSpec((192, C), lambda i, m: (half(m), 0)),
        pl.BlockSpec((192, 3 * C), lambda i, m: (half(m), 0)),
        pl.BlockSpec((192, C), lambda i, m: (half(m), 0)),
        pl.BlockSpec((C, HID // 2), lambda i, m: (0, half(m))),
        pl.BlockSpec((3, 3, 3, HID // 2), lambda i, m: (0, 0, 0, half(m))),
        pl.BlockSpec((HID // 2, C), lambda i, m: (half(m), 0)),
    ]
    if own:
        out_shape += [shape((C,), F32), shape((C,), F32), shape((6,), F32), shape((6,), F32)]
        out_specs += [pl.BlockSpec((C,), lambda i, m: (0,))] * 2 + [pl.BlockSpec(memory_space=pltpu.SMEM)] * 2
    return pl.pallas_call(
        functools.partial(unpack_kernel, own),
        out_shape=tuple(out_shape),
        grid_spec=pltpu.PrefetchScalarGridSpec(
            num_scalar_prefetch=1,
            grid=(1,),
            in_specs=[pl.BlockSpec((STACK, 128), lambda i, m: (0, 0))]
            + [pl.BlockSpec(memory_space=pl.ANY)] * len(partial),
            out_specs=tuple(out_specs),
        ),
        input_output_aliases={2 + i: i for i in range(len(partial))},
        name="unpack_own" if own else "unpack_other",
    )(me, gathered, *partial)


def local(
    tokens, out_grad, first_gain, depth_qkv, depth_out, time_qkv, time_out, second_gain, up_weight,
    spatial_kernel, down_weight, depth_scale, time_scale,
):
    me = jnp.stack([lax.axis_index(TA), lax.axis_index(DEV), lax.axis_index("core")]).astype(jnp.int32)
    block_shape = tokens.shape
    flat = tokens.reshape(ROWS, C)
    og = out_grad.reshape(ROWS, C)
    count, frames = lax.axis_size(DEV), lax.axis_size(TA)
    ahead = [(i, i + 1) for i in range(count - 1)]
    behind = [(i + 1, i) for i in range(count - 1)]

    def turned(parts, axes, size):
        return [
            lax.ppermute(part, axes, [(i, (i + step) % size) for i in range(size)]) if step else part
            for step, part in enumerate(parts)
        ]

    queue = []

    def exchange(values, axes):
        if queue:
            values, _ = lax.optimization_barrier((values, queue[-1]))
        queue.append(lax.all_to_all(values, axes, split_axis=0, concat_axis=0, tiled=True))
        return queue[-1]

    dep, tim = first_norm(flat, first_gain)
    tim = exchange(tim, TA)
    dep = exchange(dep, DEV)
    tim_out, tim_fields, tim_mixed = attend(tim, time_qkv, time_out, time_scale)
    tim_back = exchange(tim_out, TA)
    dep_out, dep_fields, dep_mixed = attend(dep, depth_qkv, depth_out, depth_scale)
    dep_back = exchange(dep_out, DEV)
    og_low = lax.ppermute(og[CELLS:], DEV, ahead)
    og_high = lax.ppermute(og[:CELLS], DEV, behind)
    dep_back, og_low, og_high = lax.optimization_barrier((dep_back, og_low, og_high))
    mid = middle_of(flat, dep_back, tim_back)
    low = lax.ppermute(mid, DEV, ahead)
    high = lax.ppermute(mid, DEV, behind)
    block_out, mgrad, bdep, btim, *saved = feed_forward(
        low, mid, high, og_low, og, og_high, second_gain, up_weight, spatial_kernel, down_weight
    )
    ffn_g = feed_grads(og, *saved, up_weight, second_gain)
    btim = exchange(btim, TA)
    bdep = exchange(bdep, DEV)
    ffn_other = swapped(ffn_g)
    tim_first, tim_g = attend_back(me, btim, tim, tim_fields, tim_mixed, time_qkv, time_out, time_scale, first_gain)
    tim_other = swapped(tim_g)
    dep_first, dep_g = attend_back(me, bdep, dep, dep_fields, dep_mixed, depth_qkv, depth_out, depth_scale, first_gain)
    dep_other = swapped(dep_g)
    factor = 1.0 / math.sqrt(ROWS * count * frames)
    stack = pair_sum(me, [ffn_g, ffn_other, dep_g, dep_other, tim_g, tim_other])
    stack = exchange(stack.reshape(COPIES, CHUNK, 128), CHIPS)
    tim_first = turned(tim_first, TA, frames)
    spread, *tim_first = lax.optimization_barrier((chip_sum(stack, factor), *tim_first))
    dep_first = turned(dep_first, DEV, count)
    own = exchange(spread, CHIPS).reshape(STACK, 128)
    input_grad = last_norm(me, flat, dep_first, tim_first, first_gain, mgrad)
    other = swapped(own)
    *partial, first_gain_grad, second_gain_grad, depth_scale_grad, time_scale_grad = unpack(True, me, own)
    dq, do, tq, to, up_g, kern_g, down_g = unpack(False, me, other, partial)
    return (
        block_out.reshape(block_shape),
        input_grad.reshape(block_shape),
        dq,
        do,
        tq,
        to,
        up_g,
        kern_g,
        down_g,
        first_gain_grad,
        second_gain_grad,
        depth_scale_grad,
        time_scale_grad,
    )


def solution(mesh):
    fine = Mesh(mesh.devices.reshape(4, 2, 2, 2, 4), ("y", "xh", "core", "xl", "z"))
    split = P(TA, DEV, None, None)
    return jax.shard_map(
        local,
        mesh=fine,
        in_specs=(split, split) + (P(),) * 11,
        out_specs=(split, split) + (P(),) * 11,
        check_vma=False,
    )
```

```python
import functools
import math

import jax
import jax.numpy as jnp
from jax import lax
from jax.experimental import pallas as pl
from jax.experimental.pallas import tpu as pltpu
from jax.sharding import Mesh
from jax.sharding import PartitionSpec as P


C = 384
HID = 1536
PW = 24
CELLS = 144
ROWS = 288
BLOCK = 256
STEPS = HID // BLOCK
PAD = 192
DEV = ("y", "xh", "core")
TA = ("xl", "z")
CHIPS = ("y", "xh", "xl", "z")
COPIES = 64
CHUNK = 152
F32 = jnp.float32
BF16 = jnp.bfloat16
EPS = 1e-5
LIMIT = 24 << 20


def piece_of(row, size):
    return (row * (65536 // size + 1)) >> 16


def spread(size, cells):
    row = lax.broadcasted_iota(jnp.int32, (size * (CELLS // cells), 1), 0)
    owner = piece_of(row, size)
    k = row - size * owner
    token = k + cells * owner + jnp.where(k >= cells, CELLS - cells, 0)
    token = jnp.where(k < 2 * cells, token, -1)
    lane = lax.broadcasted_iota(jnp.int32, (row.shape[0], ROWS), 1)
    return jnp.where(token == lane, 1.0, 0.0).astype(BF16)


def spread_depth():
    return spread(24, 9)


def spread_time():
    return spread(40, 18)


def same_group(rows):
    def group(index):
        if rows == 320:
            return index - 40 * piece_of(index, 40)
        k = index - 24 * piece_of(index, 24)
        return jnp.where(k >= 9, k - 9, k) + jnp.where(k >= 18, 9, 0)

    left = group(lax.broadcasted_iota(jnp.int32, (rows, 1), 0))
    right = group(lax.broadcasted_iota(jnp.int32, (1, rows), 1))
    return jnp.where(left == right, 1.0, 0.0)


def dot(left, right, dims=((1,), (0,)), precision=None):
    return lax.dot_general(
        left, right, (dims, ((), ())), preferred_element_type=F32, precision=precision
    )


def norm_parts(values):
    centered = values - jnp.mean(values, axis=-1, keepdims=True)
    inverse = lax.rsqrt(jnp.mean(centered * centered, axis=-1, keepdims=True) + EPS)
    return centered * inverse, inverse


def norm_back(scaled, inverse, grads):
    mean = jnp.mean(grads, axis=-1, keepdims=True)
    along = jnp.mean(grads * scaled, axis=-1, keepdims=True)
    return (grads - mean - scaled * along) * inverse


def vmem(count):
    return [pl.BlockSpec(memory_space=pltpu.VMEM)] * count


SMEM = [pl.BlockSpec(memory_space=pltpu.SMEM)]


def shape(dims, kind=BF16):
    return jax.ShapeDtypeStruct(dims, kind)


def deal(values, turn, mask, part_refs, hold_ref):
    count = len(part_refs)
    hold_ref[...] = values.reshape(count, values.shape[0] // count, C)
    for step, ref in enumerate(part_refs):
        ref[...] = hold_ref[(turn + step) & mask].astype(BF16)


def row_of(ref):
    return ref[...].reshape(1, ref.shape[0])


def first_kernel(tok_ref, gain_ref, dep_ref, tim_ref):
    scaled, _ = norm_parts(tok_ref[...].astype(F32))
    normed = (scaled * row_of(gain_ref)).astype(BF16)
    dep_ref[...] = dot(spread_depth(), normed).reshape(16, 24, C).astype(BF16)
    tim_ref[...] = dot(spread_time(), normed).reshape(8, 40, C).astype(BF16)


def first_norm(tokens, gain):
    return pl.pallas_call(
        first_kernel,
        out_shape=(shape((16, 24, C)), shape((8, 40, C))),
        in_specs=vmem(2),
        out_specs=tuple(vmem(2)),
        name="first_norm",
    )(tokens, gain)


ATT = 2304


def lane_is_low():
    return lax.broadcasted_iota(jnp.int32, (1, 128), 1) < 64


def head_ones():
    row = lax.broadcasted_iota(jnp.int32, (128, 128), 0) < 64
    col = lax.broadcasted_iota(jnp.int32, (128, 128), 1) < 64
    return jnp.where(row == col, 1.0, 0.0).astype(BF16)


def head_sum(values, ones):
    high = values.astype(BF16)
    low = (values - high.astype(F32)).astype(BF16)
    return dot(high, ones) + dot(low, ones)


def joined(ref):
    count, part, _ = ref.shape
    return ref[...].astype(F32).reshape(count * part, C).astype(BF16)


def attend_kernel(in_ref, w_ref, wo_ref, scale_ref, out_ref, fields_ref, mixed_ref, same_ref):
    rowed = joined(in_ref)
    rows = rowed.shape[0]
    fields_ref[...] = dot(rowed, w_ref[...]).astype(BF16)
    same_ref[...] = same_group(rows)
    ones = head_ones()
    low = lane_is_low()
    side = jnp.ones((rows, 128), BF16)

    def one_pair(pair, _):
        at = pl.multiple_of(128 * pair, 128)
        query = fields_ref[:, pl.ds(at, 128)].astype(F32)
        keyed = fields_ref[:, pl.ds(C + at, 128)].astype(F32)
        valued = fields_ref[:, pl.ds(2 * C + at, 128)]
        query = query * lax.rsqrt(head_sum(query * query, ones) + 1e-6)
        keyed = (keyed * lax.rsqrt(head_sum(keyed * keyed, ones) + 1e-6)).astype(BF16)
        query = query * jnp.where(low, scale_ref[2 * pair], scale_ref[2 * pair + 1])
        both = jnp.concatenate([valued, side], axis=1)
        results = []
        for half in range(2):
            mine = low if half == 0 else jnp.logical_not(low)
            scores = dot(jnp.where(mine, query, 0.0).astype(BF16), keyed, ((1,), (1,)))
            weights = (jnp.exp(scores) * same_ref[...]).astype(BF16)
            sums = dot(weights, both)
            results.append(sums[:, :128] / sums[:, 128:])
        mixed_ref[:, pl.ds(at, 128)] = jnp.where(low, results[0], results[1]).astype(BF16)
        return 0

    lax.fori_loop(0, 3, one_pair, 0)
    out_ref[...] = dot(mixed_ref[...], wo_ref[...]).reshape(out_ref.shape).astype(BF16)


def attend(inputs, weight, out_weight, scale):
    rows = inputs.shape[0] * inputs.shape[1]
    return pl.pallas_call(
        attend_kernel,
        out_shape=(shape(inputs.shape), shape((rows, 3 * C)), shape((rows, C))),
        in_specs=vmem(3) + SMEM,
        out_specs=tuple(vmem(3)),
        scratch_shapes=[pltpu.VMEM((rows, rows), F32)],
    )(inputs, weight, out_weight, scale)


def put_tile(ref, tile, values):
    for half in range(2):
        ref[half, 192 * tile : 192 * tile + 192, :] = values[192 * half : 192 * half + 192].astype(BF16)


def wide(values, lanes):
    return jnp.concatenate([values] * 3, axis=1)[:, :lanes]


def attend_back_kernel(grad_ref, in_ref, me_ref, fields_ref, mixed_ref, w_ref, wo_ref, scale_ref, gain_ref, *refs):
    count = in_ref.shape[0]
    out_refs, (weights_ref, small_ref, same_ref, fg_ref, cot_ref, hold_ref) = refs[:count], refs[count:]
    grads = joined(grad_ref)
    rows = grads.shape[0]
    same_ref[...] = same_group(rows)
    out_grad = dot(mixed_ref[...], grads, ((0,), (0,)))
    for tile in range(3):
        put_tile(weights_ref, 9 + tile, out_grad[:, 128 * tile : 128 * tile + 128])
    cot_ref[...] = dot(grads, wo_ref[...], ((1,), (1,))).astype(BF16)
    ones = head_ones()
    low = lane_is_low()
    side = jnp.ones((rows, 128), BF16)
    full = jnp.ones((128, 128), BF16)
    small_ref[24:32, :] = jnp.zeros((8, 128), F32)

    def one_pair(pair, _):
        at = pl.multiple_of(128 * pair, 128)
        query = fields_ref[:, pl.ds(at, 128)].astype(F32)
        keyed = fields_ref[:, pl.ds(C + at, 128)].astype(F32)
        valued = fields_ref[:, pl.ds(2 * C + at, 128)]
        query_inv = lax.rsqrt(head_sum(query * query, ones) + 1e-6)
        keyed_inv = lax.rsqrt(head_sum(keyed * keyed, ones) + 1e-6)
        query = query * query_inv
        keyed = keyed * keyed_inv
        scale = jnp.where(low, scale_ref[2 * pair], scale_ref[2 * pair + 1])
        scaled = query * scale
        keyed_short = keyed.astype(BF16)
        cot = cot_ref[:, pl.ds(at, 128)]
        along = cot.astype(F32) * mixed_ref[:, pl.ds(at, 128)].astype(F32)
        query_grad = jnp.zeros((rows, 128), F32)
        keyed_grad = jnp.zeros((rows, 128), F32)
        value_grad = jnp.zeros((rows, 128), F32)
        for half in range(2):
            mine = low if half == 0 else jnp.logical_not(low)
            delta = wide(head_sum(jnp.where(mine, along, 0.0), full), rows)
            mine_query = jnp.where(mine, scaled, 0.0).astype(BF16)
            mine_cot = jnp.where(mine, cot.astype(F32), 0.0).astype(BF16)
            mine_keyed = jnp.where(mine, keyed, 0.0).astype(BF16)
            scores = dot(mine_query, keyed_short, ((1,), (1,)))
            weights = jnp.exp(scores) * same_ref[...]
            total = dot(weights.astype(BF16), side)
            weights = weights * wide(1.0 / total, rows)
            weights_grad = dot(mine_cot, valued, ((1,), (1,)))
            scores_grad = (weights * (weights_grad - delta)).astype(BF16)
            value_grad = value_grad + dot(weights.astype(BF16), mine_cot, ((0,), (0,)))
            query_grad = query_grad + dot(scores_grad, mine_keyed)
            keyed_grad = keyed_grad + dot(scores_grad, mine_query, ((0,), (0,)))
        total = jnp.sum(query_grad * query, axis=0, keepdims=True)
        small_ref[pl.ds(24 + pair, 1), :] = head_sum(jnp.broadcast_to(total, (8, 128)), ones)[:1]
        query_grad = query_grad * scale
        query_grad = (query_grad - query * head_sum(query * query_grad, ones)) * query_inv
        keyed_grad = (keyed_grad - keyed * head_sum(keyed * keyed_grad, ones)) * keyed_inv
        fg_ref[:, pl.ds(at, 128)] = query_grad.astype(BF16)
        fg_ref[:, pl.ds(C + at, 128)] = keyed_grad.astype(BF16)
        fg_ref[:, pl.ds(2 * C + at, 128)] = value_grad.astype(BF16)
        return 0

    lax.fori_loop(0, 3, one_pair, 0)
    back = dot(fg_ref[...], w_ref[...], ((1,), (1,)))
    deal(back, me_ref[count // 8 - 1], count - 1, out_refs, hold_ref)
    rowed = joined(in_ref)
    grad = dot(rowed, fg_ref[...], ((0,), (0,)))
    for tile in range(9):
        put_tile(weights_ref, tile, grad[:, 128 * tile : 128 * tile + 128])
    gain_part = jnp.sum(back * rowed.astype(F32), axis=0, keepdims=True) / row_of(gain_ref)
    small_ref[0:24, :] = jnp.zeros((24, 128), F32)
    for tile in range(3):
        small_ref[8 * tile : 8 * tile + 1, :] = gain_part[:, 128 * tile : 128 * tile + 128]
    for half in range(2):
        weights_ref[half, ATT:, :] = small_ref[...].astype(BF16)


def attend_back(me, grads, inputs, fields, mixed, weight, out_weight, scale, gain):
    count, part, _ = inputs.shape
    rows = count * part
    outs = pl.pallas_call(
        attend_back_kernel,
        out_shape=(shape((part, C)),) * count + (shape((2, ATT + 32, 128)),),
        in_specs=vmem(2) + SMEM + vmem(4) + SMEM + vmem(1),
        out_specs=tuple(vmem(count + 1)),
        scratch_shapes=[
            pltpu.VMEM((32, 128), F32),
            pltpu.VMEM((rows, rows), F32),
            pltpu.VMEM((rows, 3 * C), BF16),
            pltpu.VMEM((rows, C), BF16),
            pltpu.VMEM((count, part, C), F32),
        ],
    )(grads, inputs, me, fields, mixed, weight, out_weight, scale, gain)
    return outs[:count], outs[count]


def middle_kernel(tok_ref, dep_ref, tim_ref, out_ref):
    total = tok_ref[...].astype(F32) + dot(spread_depth(), joined(dep_ref), ((0,), (0,)))
    out_ref[...] = (total + dot(spread_time(), joined(tim_ref), ((0,), (0,)))).astype(BF16)


def middle_of(tokens, depth, time):
    return pl.pallas_call(
        middle_kernel,
        out_shape=shape((ROWS, C)),
        in_specs=vmem(3),
        out_specs=vmem(1)[0],
        name="middle",
    )(tokens, depth, time)


STRIDE = 1600
FFN = 3 * STRIDE


def down_one(values, first):
    return jnp.where(first, 0.0, pltpu.roll(values, 1, 0))


def up_one(values, last):
    return jnp.where(last, 0.0, pltpu.roll(values, PW - 1, 0))


def act_pair(values):
    square = values * values
    inner = 0.7978845608 * values * (1.0 + 0.044715 * square)
    tanh = jnp.tanh(inner)
    half = 0.5 * (1.0 + tanh)
    slope = 0.7978845608 * (1.0 + 3.0 * 0.044715 * square)
    return values * half, half + 0.5 * values * (1.0 - tanh * tanh) * slope


def feed_kernel(
    low_ref, mid_ref, high_ref, og_low_ref, og_ref, og_high_ref, gain_ref, up_ref, kern_ref, down_ref,
    block_ref, mgrad_ref, bdep_ref, btim_ref, own_ref, hid_out, fgr_out, act_out, hgr_out,
    norm_ref, og4_ref, hid_ref, fgr_ref, act_ref, hgr_ref, ag_ref, block_acc, back_acc,
):
    step = pl.program_id(0)

    @pl.when(step == 0)
    def _():
        for at, ref in ((0, low_ref), (ROWS, mid_ref), (2 * ROWS, high_ref)):
            scaled, _ = norm_parts(ref[...].astype(F32))
            norm_ref[at : at + ROWS, :] = (scaled * row_of(gain_ref)).astype(BF16)
        og4_ref[0:CELLS, :] = og_low_ref[...]
        og4_ref[CELLS : CELLS + ROWS, :] = og_ref[...]
        og4_ref[CELLS + ROWS : 2 * ROWS, :] = og_high_ref[...]
        hid_ref[...] = jnp.zeros(hid_ref.shape, F32)
        fgr_ref[...] = jnp.zeros(fgr_ref.shape, F32)
        block_acc[...] = jnp.zeros(block_acc.shape, F32)
        back_acc[...] = jnp.zeros(back_acc.shape, F32)
        own_ref[...] = norm_ref[ROWS : 2 * ROWS, :]

    place = lax.broadcasted_iota(jnp.int32, (PW, 128), 0)
    first, last = place == 0, place == PW - 1
    short = dot(norm_ref[...], up_ref[...]).astype(BF16)
    hid_out[...] = short[CELLS : 5 * CELLS]
    hidden = short.astype(F32)
    ag_ref[...] = dot(og4_ref[...], down_ref[...], ((1,), (1,)))
    for lt in range(2):
        for piece in range(6):
            hid_ref[lt, piece * PAD + PW : piece * PAD + PW + CELLS, :] = hidden[
                piece * CELLS : (piece + 1) * CELLS, 128 * lt : 128 * lt + 128
            ]

    for lt in range(2):
        lanes = slice(128 * lt, 128 * lt + 128)

        def forward(piece, _, lt=lt, lanes=lanes):
            for i in range(6):
                acc = [None] * 3
                for a in range(3):
                    for b in range(3):
                        start = pl.multiple_of((piece + a) * PAD + PW * (i + b), 8)
                        window = hid_ref[lt, pl.ds(start, PW), :]
                        for e in range(3):
                            term = kern_ref[a, b, e : e + 1, lanes] * window
                            acc[e] = term if acc[e] is None else acc[e] + term
                filtered = acc[1] + down_one(acc[0], first) + up_one(acc[2], last)
                value, slope = act_pair(filtered)
                at = pl.multiple_of(piece * CELLS + PW * i, 8)
                grad = (ag_ref[pl.ds(at, PW), lanes] * slope).astype(BF16).astype(F32)
                fgr_ref[lt, pl.ds(pl.multiple_of(piece * PAD + PW * (i + 1), 8), PW), :] = grad
                act_ref[pl.ds(at, PW), lanes] = value
            return 0

        lax.fori_loop(0, 4, forward, 0)

        def backward(piece, sums, lt=lt, lanes=lanes):
            sums = list(sums)
            for i in range(6):
                acc = [None] * 3
                for a in range(3):
                    for b in range(3):
                        start = pl.multiple_of((piece + 2 - a) * PAD + PW * (i + 2 - b), 8)
                        window = fgr_ref[lt, pl.ds(start, PW), :]
                        for e in range(3):
                            term = kern_ref[a, b, e : e + 1, lanes] * window
                            acc[e] = term if acc[e] is None else acc[e] + term
                total = acc[1] + up_one(acc[0], last) + down_one(acc[2], first)
                hgr_ref[pl.ds(pl.multiple_of(piece * CELLS + PW * i, 8), PW), lanes] = total
            return tuple(sums)

        lax.fori_loop(0, 2, backward, ())

    for lt in range(2):
        for piece in range(2):
            at = (piece + 1) * PAD + PW
            fgr_out[piece * CELLS : piece * CELLS + CELLS, 128 * lt : 128 * lt + 128] = fgr_ref[
                lt, at : at + CELLS, :
            ].astype(BF16)
    active = act_ref[CELLS : CELLS + ROWS, :].astype(BF16)
    act_out[...] = active
    block_acc[...] += dot(active, down_ref[...])
    hidden_grad = hgr_ref[...].astype(BF16)
    hgr_out[...] = hidden_grad
    back_acc[...] += dot(hidden_grad, up_ref[...], ((1,), (1,)))

    @pl.when(step == STEPS - 1)
    def _():
        wide = mid_ref[...].astype(F32)
        block_ref[...] = (wide + block_acc[...]).astype(BF16)
        scaled, inverse = norm_parts(wide)
        back = norm_back(scaled, inverse, back_acc[...] * row_of(gain_ref))
        middle_grad = og_ref[...].astype(F32) + back
        mgrad_ref[...] = middle_grad
        short = middle_grad.astype(BF16)
        bdep_ref[...] = dot(spread_depth(), short).reshape(16, 24, C).astype(BF16)
        btim_ref[...] = dot(spread_time(), short).reshape(8, 40, C).astype(BF16)


def grads_kernel(
    og_ref, own_ref, hid_in, fgr_in, act_in, hgr_in, up_ref, gain_ref, weights_ref, hid_ref, fgr_ref, prod_acc, kgrad_ref
):
    step = pl.program_id(0)

    @pl.when(step == 0)
    def _():
        hid_ref[...] = jnp.zeros(hid_ref.shape, F32)
        prod_acc[...] = jnp.zeros(prod_acc.shape, F32)

    place = lax.broadcasted_iota(jnp.int32, (PW, 128), 0)
    first, last = place == 0, place == PW - 1
    for lt in range(2):
        lanes = slice(128 * lt, 128 * lt + 128)
        fgr_ref[lt] = fgr_in[:, lanes].astype(F32)
        for piece in range(4):
            hid_ref[lt, piece * PAD + PW : piece * PAD + PW + CELLS, :] = hid_in[
                piece * CELLS : piece * CELLS + CELLS, lanes
            ].astype(F32)

    for lt in range(2):
        for a in range(3):

            def products(piece, sums, a=a, lt=lt):
                sums = list(sums)
                for i in range(6):
                    own = pl.multiple_of(piece * CELLS + PW * i, 8)
                    grad = fgr_ref[lt, pl.ds(own, PW), :]
                    shifted = (up_one(grad, last), grad, down_one(grad, first))
                    for b in range(3):
                        start = pl.multiple_of((piece + a) * PAD + PW * (i + b), 8)
                        window = hid_ref[lt, pl.ds(start, PW), :]
                        for e in range(3):
                            term = window * shifted[e]
                            k = 3 * b + e
                            sums[k] = sums[k] + (term[0:8] + term[8:16] + term[16:24])
                return tuple(sums)

            sums = lax.fori_loop(0, 2, products, tuple(jnp.zeros((8, 128), F32) for _ in range(9)))
            for k in range(9):
                row = 32 * lt + 9 * a + k
                kgrad_ref[row : row + 1, :] = jnp.sum(sums[k], axis=0, keepdims=True)
        kgrad_ref[32 * lt + 27 : 32 * lt + 32, :] = jnp.zeros((5, 128), F32)

    down_grad = dot(act_in[...], og_ref[...], ((0,), (0,)))
    up_grad = dot(own_ref[...], hgr_in[...], ((0,), (0,)))
    product = up_grad * up_ref[...].astype(F32)
    prod_acc[...] += product[:, :128] + product[:, 128:]
    half = step // 3
    base = pl.multiple_of((step - 3 * half) * STRIDE, 16)
    for tile in range(2):
        weights_ref[half, pl.ds(base + C * tile, C), :] = up_grad[:, 128 * tile : 128 * tile + 128].astype(BF16)
    for tile in range(3):
        at = 2 * C + BLOCK * tile
        weights_ref[half, pl.ds(base + at, BLOCK), :] = down_grad[:, 128 * tile : 128 * tile + 128].astype(BF16)
    weights_ref[half, pl.ds(base + 1536, 64), :] = kgrad_ref[...].astype(BF16)

    @pl.when(step == STEPS - 1)
    def _():
        part = dot(jnp.ones((8, 128), F32), prod_acc[...], ((1,), (1,)), lax.Precision.HIGHEST)
        part = part / row_of(gain_ref)
        for tile in range(3):
            kgrad_ref[8 * tile : 8 * tile + 8, :] = part[:, 128 * tile : 128 * tile + 128]
        kgrad_ref[24:32, :] = jnp.zeros((8, 128), F32)
        for side in range(2):
            weights_ref[side, 3 * STRIDE :, :] = kgrad_ref[0:32, :].astype(BF16)


def feed_grads(og, own, hid, fgr, act, hgr, up, gain):
    def column(rows):
        return pl.BlockSpec((rows, BLOCK), lambda s: (0, s))

    return pl.pallas_call(
        grads_kernel,
        grid=(STEPS,),
        out_shape=shape((2, FFN + 32, 128)),
        in_specs=[
            pl.BlockSpec((ROWS, C), lambda s: (0, 0)),
            pl.BlockSpec((ROWS, C), lambda s: (0, 0)),
            column(2 * ROWS),
            column(ROWS),
            column(ROWS),
            column(ROWS),
            column(C),
            pl.BlockSpec((C,), lambda s: (0,)),
        ],
        out_specs=pl.BlockSpec((2, FFN + 32, 128), lambda s: (0, 0, 0)),
        scratch_shapes=[
            pltpu.VMEM((2, 4 * PAD, 128), F32),
            pltpu.VMEM((2, ROWS, 128), F32),
            pltpu.VMEM((C, 128), F32),
            pltpu.VMEM((64, 128), F32),
        ],
        name="feed_grads",
    )(og, own, hid, fgr, act, hgr, up, gain)


def feed_forward(low, mid, high, og_low, og, og_high, gain, up, kern, down):
    def whole(*dims):
        return pl.BlockSpec(dims, lambda s: (0,) * len(dims))

    return pl.pallas_call(
        feed_kernel,
        grid=(STEPS,),
        out_shape=(
            shape((ROWS, C)),
            shape((ROWS, C), F32),
            shape((16, 24, C)),
            shape((8, 40, C)),
            shape((ROWS, C)),
            shape((2 * ROWS, HID)),
            shape((ROWS, HID)),
            shape((ROWS, HID)),
            shape((ROWS, HID)),
        ),
        in_specs=[
            whole(ROWS, C),
            whole(ROWS, C),
            whole(ROWS, C),
            whole(CELLS, C),
            whole(ROWS, C),
            whole(CELLS, C),
            whole(C),
            pl.BlockSpec((C, BLOCK), lambda s: (0, s)),
            pl.BlockSpec((3, 3, 3, BLOCK), lambda s: (0, 0, 0, s)),
            pl.BlockSpec((BLOCK, C), lambda s: (s, 0)),
        ],
        out_specs=(
            whole(ROWS, C),
            whole(ROWS, C),
            whole(16, 24, C),
            whole(8, 40, C),
            whole(ROWS, C),
            pl.BlockSpec((2 * ROWS, BLOCK), lambda s: (0, s)),
            pl.BlockSpec((ROWS, BLOCK), lambda s: (0, s)),
            pl.BlockSpec((ROWS, BLOCK), lambda s: (0, s)),
            pl.BlockSpec((ROWS, BLOCK), lambda s: (0, s)),
        ),
        scratch_shapes=[
            pltpu.VMEM((3 * ROWS, C), BF16),
            pltpu.VMEM((2 * ROWS, C), BF16),
            pltpu.VMEM((2, 6 * PAD, 128), F32),
            pltpu.VMEM((2, 4 * PAD, 128), F32),
            pltpu.VMEM((2 * ROWS, BLOCK), F32),
            pltpu.VMEM((ROWS, BLOCK), F32),
            pltpu.VMEM((2 * ROWS, BLOCK), F32),
            pltpu.VMEM((ROWS, C), F32),
            pltpu.VMEM((ROWS, C), F32),
        ],
        name="feed_forward",
    )(low, mid, high, og_low, og, og_high, gain, up, kern, down)


def last_kernel(me_ref, tok_ref, gain_ref, mgrad_ref, *rest):
    dep_refs, tim_refs, (out_ref, dep_hold, tim_hold) = rest[:16], rest[16:24], rest[24:]
    for step, ref in enumerate(dep_refs):
        dep_hold[(me_ref[1] - step) & 15] = ref[...].astype(F32)
    for step, ref in enumerate(tim_refs):
        tim_hold[(me_ref[0] - step) & 7] = ref[...].astype(F32)
    dep = dep_hold[...].reshape(384, C).astype(BF16)
    tim = tim_hold[...].reshape(320, C).astype(BF16)
    back = dot(spread_depth(), dep, ((0,), (0,))) + dot(spread_time(), tim, ((0,), (0,)))
    scaled, inverse = norm_parts(tok_ref[...].astype(F32))
    out_ref[...] = (mgrad_ref[...] + norm_back(scaled, inverse, back * row_of(gain_ref))).astype(BF16)


def last_norm(me, tokens, depth, time, gain, mgrad):
    return pl.pallas_call(
        last_kernel,
        out_shape=shape((ROWS, C)),
        in_specs=SMEM + vmem(27),
        out_specs=vmem(1)[0],
        scratch_shapes=[pltpu.VMEM((16, 24, C), F32), pltpu.VMEM((8, 40, C), F32)],
        compiler_params=pltpu.CompilerParams(vmem_limit_bytes=LIMIT),
        name="last_norm",
    )(me, tokens, gain, mgrad, *depth, *time)


STACK = COPIES * CHUNK
DEP = FFN + 32
TIM = DEP + ATT + 32


def pair_kernel(me_ref, *refs):
    out_ref, at = refs[-1], 0
    for one, two in zip(refs[0:-1:2], refs[1:-1:2], strict=True):
        size = one.shape[1]
        out_ref[at : at + size, :] = (one[0].astype(F32) + two[0].astype(F32)).astype(BF16)
        at += size
    out_ref[at:, :] = jnp.zeros((STACK - at, 128), BF16)


def swapped(array):
    return lax.ppermute(array, "core", [(0, 1), (1, 0)])


def pair_sum(me, args):
    return pl.pallas_call(
        pair_kernel,
        out_shape=shape((STACK, 128)),
        grid_spec=pltpu.PrefetchScalarGridSpec(
            num_scalar_prefetch=1,
            grid=(1,),
            in_specs=[pl.BlockSpec((1,) + a.shape[1:], lambda i, m: (m[2], 0, 0)) for a in args],
            out_specs=pl.BlockSpec((STACK, 128), lambda i, m: (0, 0)),
        ),
        compiler_params=pltpu.CompilerParams(vmem_limit_bytes=LIMIT),
    )(me, *args)


def chip_kernel(factor, in_ref, out_ref):
    def add(source, total):
        return total + in_ref[source].astype(F32)

    total = lax.fori_loop(1, COPIES, add, in_ref[0].astype(F32), unroll=3)
    total = (total * factor).astype(BF16)

    def put(target, _):
        out_ref[target] = total
        return 0

    lax.fori_loop(0, COPIES, put, 0, unroll=2)


def chip_sum(received, factor):
    return pl.pallas_call(
        functools.partial(chip_kernel, factor),
        out_shape=shape(received.shape),
        in_specs=vmem(1),
        out_specs=vmem(1)[0],
        compiler_params=pltpu.CompilerParams(vmem_limit_bytes=LIMIT),
        name="chip_sum",
    )(received)


def unpack_kernel(own, me_ref, in_ref, *refs):
    refs = refs if own else refs[7:]
    dq_ref, do_ref, tq_ref, to_ref, up_ref, kg_ref, dn_ref = refs[:7]
    for step in range(3):
        at = STRIDE * step
        for tile in range(2):
            lanes = slice(BLOCK * step + 128 * tile, BLOCK * step + 128 * tile + 128)
            up_ref[:, lanes] = in_ref[at + C * tile : at + C * tile + C, :].astype(F32)
            kgrad = in_ref[at + 1536 + 32 * tile : at + 1568 + 32 * tile, :].astype(F32)
            for k in range(27):
                kg_ref[k // 9, k // 3 % 3, k % 3 : k % 3 + 1, lanes] = kgrad[k : k + 1]
        for tile in range(3):
            rows = in_ref[at + 768 + BLOCK * tile : at + 1024 + BLOCK * tile, :].astype(F32)
            dn_ref[BLOCK * step : BLOCK * step + BLOCK, 128 * tile : 128 * tile + 128] = rows
    for base, q_ref, o_ref in ((DEP, dq_ref, do_ref), (TIM, tq_ref, to_ref)):
        for tile in range(12):
            rows = in_ref[base + 192 * tile : base + 192 * tile + 192, :].astype(F32)
            if tile < 9:
                q_ref[:, 128 * tile : 128 * tile + 128] = rows
            else:
                o_ref[:, 128 * (tile - 9) : 128 * (tile - 9) + 128] = rows
    if own:
        first_ref, second_ref, dscale_ref, tscale_ref = refs[7:11]
        two = in_ref[FFN : FFN + 32, :].astype(F32)
        dep = in_ref[DEP + ATT : DEP + ATT + 32, :].astype(F32)
        tim = in_ref[TIM + ATT : TIM + ATT + 32, :].astype(F32)
        one = dep + tim
        for tile in range(3):
            lanes = slice(128 * tile, 128 * tile + 128)
            second_ref[lanes] = two[8 * tile : 8 * tile + 1].reshape(128)
            first_ref[lanes] = one[8 * tile : 8 * tile + 1].reshape(128)
        for head in range(6):
            dscale_ref[head] = dep[24 + head // 2, 64 * (head % 2)]
            tscale_ref[head] = tim[24 + head // 2, 64 * (head % 2)]


def unpack(own, me, gathered, partial=()):
    half = (lambda m: m[2]) if own else (lambda m: 1 - m[2])
    out_shape = [
        shape((C, 3 * C), F32),
        shape((C, C), F32),
        shape((C, 3 * C), F32),
        shape((C, C), F32),
        shape((C, HID), F32),
        shape((3, 3, 3, HID), F32),
        shape((HID, C), F32),
    ]
    out_specs = [
        pl.BlockSpec((192, 3 * C), lambda i, m: (half(m), 0)),
        pl.BlockSpec((192, C), lambda i, m: (half(m), 0)),
        pl.BlockSpec((192, 3 * C), lambda i, m: (half(m), 0)),
        pl.BlockSpec((192, C), lambda i, m: (half(m), 0)),
        pl.BlockSpec((C, HID // 2), lambda i, m: (0, half(m))),
        pl.BlockSpec((3, 3, 3, HID // 2), lambda i, m: (0, 0, 0, half(m))),
        pl.BlockSpec((HID // 2, C), lambda i, m: (half(m), 0)),
    ]
    if own:
        out_shape += [shape((C,), F32), shape((C,), F32), shape((6,), F32), shape((6,), F32)]
        out_specs += [pl.BlockSpec((C,), lambda i, m: (0,))] * 2 + [pl.BlockSpec(memory_space=pltpu.SMEM)] * 2
    return pl.pallas_call(
        functools.partial(unpack_kernel, own),
        out_shape=tuple(out_shape),
        grid_spec=pltpu.PrefetchScalarGridSpec(
            num_scalar_prefetch=1,
            grid=(1,),
            in_specs=[pl.BlockSpec((STACK, 128), lambda i, m: (0, 0))]
            + [pl.BlockSpec(memory_space=pl.ANY)] * len(partial),
            out_specs=tuple(out_specs),
        ),
        input_output_aliases={2 + i: i for i in range(len(partial))},
        compiler_params=pltpu.CompilerParams(vmem_limit_bytes=LIMIT),
        name="unpack_own" if own else "unpack_other",
    )(me, gathered, *partial)


def local(
    tokens, out_grad, first_gain, depth_qkv, depth_out, time_qkv, time_out, second_gain, up_weight,
    spatial_kernel, down_weight, depth_scale, time_scale,
):
    me = jnp.stack([lax.axis_index(TA), lax.axis_index(DEV), lax.axis_index("core")]).astype(jnp.int32)
    block_shape = tokens.shape
    flat = tokens.reshape(ROWS, C)
    og = out_grad.reshape(ROWS, C)
    count, frames = lax.axis_size(DEV), lax.axis_size(TA)
    ahead = [(i, i + 1) for i in range(count - 1)]
    behind = [(i + 1, i) for i in range(count - 1)]

    def turned(parts, axes, size):
        return [
            lax.ppermute(part, axes, [(i, (i + step) % size) for i in range(size)]) if step else part
            for step, part in enumerate(parts)
        ]

    queue = []

    def exchange(values, axes):
        if queue:
            values, _ = lax.optimization_barrier((values, queue[-1]))
        queue.append(lax.all_to_all(values, axes, split_axis=0, concat_axis=0, tiled=True))
        return queue[-1]

    dep, tim = first_norm(flat, first_gain)
    tim = exchange(tim, TA)
    dep = exchange(dep, DEV)
    tim_out, tim_fields, tim_mixed = attend(tim, time_qkv, time_out, time_scale)
    tim_back = exchange(tim_out, TA)
    dep_out, dep_fields, dep_mixed = attend(dep, depth_qkv, depth_out, depth_scale)
    dep_back = exchange(dep_out, DEV)
    og_low = lax.ppermute(og[CELLS:], DEV, ahead)
    og_high = lax.ppermute(og[:CELLS], DEV, behind)
    dep_back, og_low, og_high = lax.optimization_barrier((dep_back, og_low, og_high))
    mid = middle_of(flat, dep_back, tim_back)
    low = lax.ppermute(mid, DEV, ahead)
    high = lax.ppermute(mid, DEV, behind)
    block_out, mgrad, bdep, btim, *saved = feed_forward(
        low, mid, high, og_low, og, og_high, second_gain, up_weight, spatial_kernel, down_weight
    )
    ffn_g = feed_grads(og, *saved, up_weight, second_gain)
    btim = exchange(btim, TA)
    bdep = exchange(bdep, DEV)
    ffn_other = swapped(ffn_g)
    tim_first, tim_g = attend_back(me, btim, tim, tim_fields, tim_mixed, time_qkv, time_out, time_scale, first_gain)
    tim_other = swapped(tim_g)
    dep_first, dep_g = attend_back(me, bdep, dep, dep_fields, dep_mixed, depth_qkv, depth_out, depth_scale, first_gain)
    dep_other = swapped(dep_g)
    factor = 1.0 / math.sqrt(ROWS * count * frames)
    stack = pair_sum(me, [ffn_g, ffn_other, dep_g, dep_other, tim_g, tim_other])
    stack = exchange(stack.reshape(COPIES, CHUNK, 128), CHIPS)
    tim_first = turned(tim_first, TA, frames)
    spread, *tim_first = lax.optimization_barrier((chip_sum(stack, factor), *tim_first))
    dep_first = turned(dep_first, DEV, count)
    own = exchange(spread, CHIPS).reshape(STACK, 128)
    input_grad = last_norm(me, flat, dep_first, tim_first, first_gain, mgrad)
    other = swapped(own)
    *partial, first_gain_grad, second_gain_grad, depth_scale_grad, time_scale_grad = unpack(True, me, own)
    dq, do, tq, to, up_g, kern_g, down_g = unpack(False, me, other, partial)
    return (
        block_out.reshape(block_shape),
        input_grad.reshape(block_shape),
        dq,
        do,
        tq,
        to,
        up_g,
        kern_g,
        down_g,
        first_gain_grad,
        second_gain_grad,
        depth_scale_grad,
        time_scale_grad,
    )


def solution(mesh):
    fine = Mesh(mesh.devices.reshape(4, 2, 2, 2, 4), ("y", "xh", "core", "xl", "z"))
    split = P(TA, DEV, None, None)
    return jax.shard_map(
        local,
        mesh=fine,
        in_specs=(split, split) + (P(),) * 11,
        out_specs=(split, split) + (P(),) * 11,
        check_vma=False,
    )
```
